32 devices in a mesh: groups: 2 (over x), ctx: 16 (over z, y, core).
Axes of the slice: x: 2, y: 2, z: 4, core: 2. Of those that a mesh axis runs over, the one named last changes fastest.
Arguments:
- events: bfloat16 [16384, 1024], P(('groups', 'ctx')), parts along dimension 0, may hold values from -6 to 6
- w_in: bfloat16 [1024, 4096], replicated, may hold values from -0.1875 to 0.1875
- w_out: bfloat16 [1024, 1024], replicated, may hold values from -0.1875 to 0.1875
- rel_bias: float32 [16, 16], replicated, may hold values from -3 to 3
- lengths: int32 [8], P('groups'), parts along dimension 0, may hold values from 1 to 4096, as said below
- block_lists: int32 [32, 2], P(('groups', 'ctx')), parts along dimension 0, may hold values from 1 to 4, as said below
- candidates: int32 [32, 128], P('groups'), parts along dimension 0, may hold values from 0 to 8191, as said below
Outputs:
- layer_output: bfloat16 [16384, 1024], P(('groups', 'ctx')), parts along dimension 0
- next_score: float32 [16384], P(('groups', 'ctx')), parts along dimension 0
- candidate_score_table: float32 [16384, 128], P(('groups', 'ctx')), parts along dimension 0
The draws below stay inside these ranges and needn't reach their ends.
There are 2 independent parts, one for each index of `groups`. The reference program is written for one: setup_inputs(seed, part) draws one part's arguments, and reference() takes and returns one part's arrays. A program takes and returns all parts, laid end to end along the dimension named above; an argument that names none is the same for every part. Nothing has to cross between parts.
Inputs may be any that keep to these rules, and one draw needn't show every extreme that they name: `lengths`: the first user has exactly 4096 events. `block_lists`: each row holds 2 different distances; row 0 lists distance 1. `candidates`: of one row's 128 rows at most 16 lie in one block, and exactly 16 in some block.
All inputs are finite; a program needn't handle non-finite values.
Results may differ from the reference program's by a relative error of at most 0.007.
Values may be sent and summed in bfloat16 or wider, within the bound.
No kernel may reach another device: no remote copies, remote signals or barrier semaphores. Data moves between devices by JAX's collectives and lax.ppermute only.
A program may use at most 128 MiB of HBM per device.

```python
import jax
import jax.numpy as jnp
from jax import lax

HEADS = 16
D = 1024
ROWS = 512
SPAN = 4
NSEL = 2
NB = 16
NCAND = 128
TOKENS = 8192
USERS = 4
MOSTLEN = 4096


def draw_lengths(key, part):
    rest_total = TOKENS - MOSTLEN
    cut_count = USERS - 2
    cuts = jnp.sort(jax.random.permutation(key, rest_total - 1)[:cut_count] + 1).astype(jnp.int32)
    bounds = jnp.concatenate([jnp.zeros((1,), jnp.int32), cuts, jnp.full((1,), rest_total, jnp.int32)])
    others = bounds[1:] - bounds[:-1]
    return jnp.concatenate([jnp.full((1,), MOSTLEN, jnp.int32), others]).astype(jnp.int32)


def draw_block_lists(key, part):
    total_block_count = TOKENS // ROWS
    row_keys = jax.random.split(key, total_block_count + 1)
    chosen = jax.random.randint(row_keys[total_block_count], (), 1, total_block_count)

    def one_row(row_key, row_num):
        shuffled = jax.random.permutation(row_key, SPAN)
        start_at = jnp.argmax((shuffled == SPAN - 1).astype(jnp.int32))
        turned = jnp.roll(shuffled, -start_at)
        shuffled_first = jnp.where(row_num == chosen, turned, shuffled)
        zero_at = jnp.argmax((shuffled == 0).astype(jnp.int32))
        zero_first = jnp.roll(shuffled, -zero_at)
        shuffled_first = jnp.where(row_num == 0, zero_first, shuffled_first)
        return shuffled_first[:NSEL] + 1
    return jax.vmap(one_row)(row_keys[:total_block_count], jnp.arange(total_block_count)).astype(jnp.int32)


def draw_candidates(key, part):
    total_block_count = TOKENS // ROWS
    slot_cap = 2 * NCAND // total_block_count
    row_keys = jax.random.split(key, total_block_count)

    def one_row(row_key):
        split_keys = jax.random.split(row_key, 4)
        full_owner = jax.random.randint(split_keys[0], (), 0, total_block_count)
        slot_list = jax.random.permutation(split_keys[1], (total_block_count - 1) * slot_cap)[:NCAND - slot_cap]
        other_owner = slot_list // slot_cap
        other_owner = other_owner + (other_owner >= full_owner).astype(jnp.int32)
        owners = jnp.concatenate([jnp.full((slot_cap,), full_owner, jnp.int32), other_owner.astype(jnp.int32)])
        owners = jax.random.permutation(split_keys[2], owners)
        local_row = jax.random.randint(split_keys[3], (NCAND,), 0, ROWS)
        return owners * ROWS + local_row
    return jax.vmap(one_row)(row_keys).astype(jnp.int32)


def level_of(own_key, shape, shards, least, largest):
    def one(position, shards_of):
        heights = jax.random.uniform(jax.random.fold_in(jax.random.fold_in(own_key, 6), position), (shards_of,), jnp.float32, least / len(shards), largest / len(shards))
        return jnp.repeat(jnp.exp(heights), shape[position] // shards_of).reshape((-1,) + (1,) * (len(shape) - position - 1))

    loudness = one(*shards[0])
    for cut in shards[1:]:
        loudness = loudness * one(*cut)
    return loudness


def bell_draw(rng, extent, scale, reach, pieces=(), kind=jnp.bfloat16):
    gain = level_of(rng, extent, pieces, -0.22, 0.18) if pieces else 1.0
    entries = jax.random.normal(rng, extent, jnp.float32) * scale * gain
    return jnp.minimum(jnp.maximum(entries, -reach), reach).astype(kind)


def setup_inputs(seed: int = 0, part: int = 0) -> dict:
    key_list = jax.random.split(jax.random.key(seed), 8)
    part_keys = jax.random.split(jax.random.fold_in(key_list[7], part), 8)
    events = bell_draw(part_keys[0], (TOKENS, D), 1.0, 6.0, ((0, 16),))
    w_in = bell_draw(key_list[1], (D, 4 * D), D ** -0.5, 0.1875)
    w_out = bell_draw(key_list[2], (D, D), D ** -0.5, 0.1875)
    rel_bias = bell_draw(key_list[3], (HEADS, NB), 1.0, 3.0, (), jnp.float32)
    lengths = draw_lengths(jax.random.fold_in(jax.random.fold_in(key_list[7], part), 71), part)
    block_lists = draw_block_lists(jax.random.fold_in(jax.random.fold_in(key_list[7], part), 71), part)
    candidates = draw_candidates(jax.random.fold_in(jax.random.fold_in(key_list[7], part), 71), part)
    return dict(events=events, w_in=w_in, w_out=w_out, rel_bias=rel_bias, lengths=lengths, block_lists=block_lists, candidates=candidates)


def layer_norm(values):
    values = values.astype(jnp.float32)
    center = values - lax.optimization_barrier(jnp.mean(values, -1, keepdims=True))
    spread = lax.optimization_barrier(jnp.mean(center * center, -1, keepdims=True))
    return center * lax.rsqrt(spread + 1e-05)

def bucket_bias(distance, rel_bias):
    buckets = rel_bias.shape[1]
    bucket = jnp.zeros(distance.shape, jnp.int32)
    for degree in range(buckets - 1):
        bucket = bucket + (distance >= 2 ** degree).astype(jnp.int32)
    rel_terms = jnp.zeros((rel_bias.shape[0],) + distance.shape, rel_bias.dtype)
    for degree in range(buckets):
        rel_terms = jnp.where((bucket == degree)[None], rel_bias[:, degree][:, None, None], rel_terms)
    return rel_terms

def user_of(positions, user_ends):
    return lax.optimization_barrier(jnp.sum((positions[:, None] >= user_ends[None, :]).astype(jnp.int32), axis=1))

def attend(queries, query_pos, query_user, key_rows, value_rows, key_pos, key_user, rel_bias):
    attention_scale = queries.shape[-1] ** (-0.5)
    scores = jnp.einsum('qhd,khd->hqk', queries.astype(jnp.float32), key_rows.astype(jnp.float32))
    distance = query_pos[:, None] - key_pos[None, :]
    rel_terms = bucket_bias(distance, rel_bias)
    allowed = (distance >= 0) & (query_user[:, None] == key_user[None, :])
    weights = jnp.where(allowed[None], jax.nn.silu(scores * attention_scale + rel_terms), 0.0).astype(jnp.bfloat16)
    return jnp.einsum('hqk,khd->qhd', weights.astype(jnp.float32), value_rows.astype(jnp.float32))

def reference(events, w_in, w_out, rel_bias, lengths, block_lists, candidates):
    total_rows, hidden_width = events.shape
    total_block_count, pick_count = block_lists.shape
    event_row_count = total_rows // total_block_count
    head_count = rel_bias.shape[0]
    head_size = hidden_width // head_count
    user_ends = jnp.cumsum(lengths).astype(jnp.int32)
    row_index = jnp.arange(total_rows, dtype=jnp.int32)
    positions = ((row_index + total_rows // 4) % total_rows).astype(jnp.int32)
    users = user_of(positions, user_ends)
    normed = layer_norm(events).astype(jnp.bfloat16)
    projected = jax.nn.silu(jnp.dot(normed, w_in, preferred_element_type=jnp.float32)).astype(jnp.bfloat16)
    gate_u = projected[:, :hidden_width]

    def shaped(columns):
        return columns.reshape(total_block_count, event_row_count, head_count, head_size)
    queries = shaped(projected[:, hidden_width:2 * hidden_width])
    value_rows = shaped(projected[:, 2 * hidden_width:3 * hidden_width])
    key_rows = shaped(projected[:, 3 * hidden_width:])
    block_pos = positions.reshape(total_block_count, event_row_count)
    block_users = users.reshape(total_block_count, event_row_count)

    def per_block(block_num):
        running = attend(queries[block_num], block_pos[block_num], block_users[block_num], key_rows[block_num], value_rows[block_num], block_pos[block_num], block_users[block_num], rel_bias)
        for pick_num in range(pick_count):
            source = ((block_num - block_lists[block_num, pick_num]) % total_block_count).astype(jnp.int32)
            running = running + attend(queries[block_num], block_pos[block_num], block_users[block_num], key_rows[source], value_rows[source], block_pos[source], block_users[source], rel_bias)
        return running
    attended = lax.map(per_block, jnp.arange(total_block_count, dtype=jnp.int32)).reshape(total_rows, hidden_width)
    gated_rows = (layer_norm(attended) * gate_u.astype(jnp.float32)).astype(jnp.bfloat16)
    layer_output = (events.astype(jnp.float32) + jnp.dot(gated_rows, w_out, preferred_element_type=jnp.float32)).astype(jnp.bfloat16)
    attention_scale = hidden_width ** (-0.5)
    following = jnp.concatenate([events[1:], events[:1]], axis=0)
    next_user = user_of(positions + 1, user_ends)
    inner = lax.optimization_barrier(jnp.sum(layer_output.astype(jnp.float32) * following.astype(jnp.float32), axis=1)) * attention_scale
    next_score = jnp.where(next_user == users, inner, 0.0)
    candidate_row_list = events[candidates]
    candidate_score_table = jnp.einsum('wza,wra->wzr', layer_output.reshape(total_block_count, event_row_count, hidden_width).astype(jnp.float32), candidate_row_list.astype(jnp.float32)) * attention_scale
    return (layer_output, next_score, candidate_score_table.reshape(total_rows, candidates.shape[1]))
```

```python
import functools

import jax
import jax.numpy as jnp
from jax import lax
from jax.experimental import pallas as pl
from jax.experimental.pallas import tpu as pltpu
from jax.sharding import PartitionSpec as P

BLOCKED = -1e9
LANES = 128
F32 = jnp.float32
BF16 = jnp.bfloat16
VMEM_BYTES = 56 * 2**20
NT = (((1,), (1,)), ((), ()))


def passed_along(value, pairs):
    return lax.ppermute(value, "ctx", pairs)


def centered(values):
    center = values - jnp.mean(values, -1, keepdims=True)
    spread = jnp.mean(center * center, -1, keepdims=True)
    return center * lax.rsqrt(spread + 1e-05)


def silu_of_half(half):
    return half * jnp.tanh(half) + half


def iota(shape, dim):
    return lax.broadcasted_iota(jnp.int32, shape, dim)


def time_base(block, count, rows):
    total = count * rows
    return lax.rem(block * rows + total // 4, total)


def starts_of(times, lengths_ref):
    end = jnp.int32(0)
    start = jnp.zeros_like(times)
    for user in range(lengths_ref.shape[0]):
        length = lengths_ref[user]
        end = end + length
        start = start + jnp.where(times >= end, length, 0)
    return start


def half_bias(rel_ref, head, bucket):
    return rel_ref[head, bucket] * 0.5


def bias_chain(distance, rel_ref, head, low, first, last):
    tile = jnp.full(distance.shape, half_bias(rel_ref, head, low), F32)
    for degree in range(first, last):
        tile = jnp.where(distance >= 2**degree, half_bias(rel_ref, head, degree + 1), tile)
    return tile


def head_rows(size, width, value):
    lane = iota((1, width), 1)
    return [
        jnp.where((lane >= size * num) & (lane < size * (num + 1)), value, 0.0).astype(BF16)
        for num in range(width // size)
    ]


def request_kernel(slot_cap, cand_ref, events_ref, out_ref):
    me = lax.axis_index("ctx")
    count, wanted = cand_ref.shape
    rows = events_ref.shape[0]
    slots = count * slot_cap
    cand = cand_ref[...]
    local = cand - me * rows
    mine = (local >= 0) & (local < rows)
    earlier = (iota((wanted, wanted), 0) < iota((wanted, wanted), 1)).astype(BF16)
    rank = jnp.dot(jnp.where(mine, 1.0, 0.0).astype(BF16), earlier, preferred_element_type=F32)
    code = jnp.where(mine, rank * rows + local.astype(F32), -1.0)
    slot_num = iota((slots, count), 0) - iota((slots, count), 1) * slot_cap
    spread = jnp.where((slot_num >= 0) & (slot_num < slot_cap), 1.0, 0.0)
    asked = jnp.dot(spread, code, preferred_element_type=F32, precision=lax.Precision.HIGHEST)
    slot = lax.rem(iota((slots, wanted), 0), slot_cap).astype(F32)
    found = asked - slot * rows
    ids = jnp.sum(jnp.where((found >= 0.0) & (found < rows), found + 1.0, 0.0), 1, keepdims=True)
    picks = (ids.astype(jnp.int32) - 1 == iota((slots, rows), 1)).astype(BF16)
    out_ref[...] = jnp.dot(picks, events_ref[...], preferred_element_type=F32).astype(BF16)


def project_kernel(events_ref, w_ref, out_ref, normed_ref):
    @pl.when(pl.program_id(0) == 0)
    def _():
        normed_ref[...] = centered(events_ref[...].astype(F32)).astype(BF16)

    value = jnp.dot(normed_ref[...], w_ref[...], preferred_element_type=F32)
    out_ref[...] = silu_of_half(0.5 * value).astype(BF16)


def own_kernel(head_size, lengths_ref, rel_ref, q_ref, v_ref, k_ref, out_ref, mask_ref):
    group = pl.program_id(0)
    rows, width = q_ref.shape
    half = rows // 2
    heads = width // head_size
    count = lax.axis_size("ctx")

    @pl.when(group == 0)
    def _():
        base = time_base(lax.axis_index("ctx"), count, rows)
        start = starts_of(base + iota((rows, LANES), 0), lengths_ref)
        for num in range(rows // LANES):
            key_time = base + num * LANES + iota((rows, LANES), 1)
            mask_ref[:, num * LANES : (num + 1) * LANES] = jnp.where(key_time >= start, 0.0, BLOCKED)

    away = iota((LANES, LANES), 0) - iota((LANES, LANES), 1)
    queries, values, keys = q_ref[...], v_ref[...], k_ref[...]
    scaled = head_rows(head_size, width, 0.5 * head_size**-0.5)
    chosen = head_rows(head_size, width, 1.0)
    parts = [([], []), ([], [])]
    for num in range(heads):
        head = group * heads + num
        tiles = [
            jnp.where(away < 0, BLOCKED, bias_chain(away, rel_ref, head, 0, 0, 7)),
            bias_chain(away + LANES, rel_ref, head, 1, 1, 8),
            jnp.where(away >= 0, half_bias(rel_ref, head, 9), half_bias(rel_ref, head, 8)),
            half_bias(rel_ref, head, 9),
        ]
        head_queries = queries * scaled[num]
        head_values = values * chosen[num]
        for part in range(2):
            seen = (part + 1) * half
            scores = lax.dot_general(
                head_queries[part * half : (part + 1) * half],
                keys[:seen],
                NT,
                preferred_element_type=F32,
            )
            lines = []
            for q_sub in range(half // LANES):
                q_tile = part * (half // LANES) + q_sub
                line = []
                for k_tile in range(seen // LANES):
                    if k_tile > q_tile:
                        line.append(jnp.zeros((LANES, LANES), BF16))
                        continue
                    part_scores = scores[
                        q_sub * LANES : (q_sub + 1) * LANES, k_tile * LANES : (k_tile + 1) * LANES
                    ]
                    mask = mask_ref[
                        q_tile * LANES : (q_tile + 1) * LANES, k_tile * LANES : (k_tile + 1) * LANES
                    ]
                    line.append(
                        silu_of_half(part_scores + tiles[q_tile - k_tile] + mask).astype(BF16)
                    )
                lines.append(jnp.concatenate(line, 1))
            parts[part][0].append(jnp.concatenate(lines, 0))
            parts[part][1].append(head_values[:seen])
    for part in range(2):
        weights = jnp.concatenate(parts[part][0], 1)
        stacked = jnp.concatenate(parts[part][1], 0)
        out_ref[part * half : (part + 1) * half] = jnp.dot(
            weights, stacked, preferred_element_type=F32
        )


def picks_kernel(chunk, last, head_size, slot_cap, *refs):
    lengths_ref, lists_ref, rel_ref, q_ref, before_ref = refs[:5]
    over_ref, far_ref, over_twin_ref, far_twin_ref, own_twin_ref, w_ref = refs[5:11]
    if last:
        gate_ref, events_ref, next_ref, flat_ref, cand_ref, w_out_ref = refs[11:17]
        layer_ref, score_ref, table_ref = refs[17:20]
        acc_ref, rows_ref, w_buf, pair_ref, mask_ref, near_ref, sems, out_buf = refs[20:]
    else:
        acc_ref = refs[11]
        rows_ref, w_buf, pair_ref, mask_ref, near_ref, sems = refs[12:]
    me = lax.axis_index("ctx")
    count = lax.axis_size("ctx")
    rows, hidden = q_ref.shape
    half = far_ref.shape[0]
    picks = lists_ref.shape[1]
    head_count, _ = rel_ref.shape
    second = lax.rem(me, 2) == 1
    shared = chunk * half

    copies = []
    for pick in range(picks):
        away = lists_ref[0, pick]
        target = rows_ref.at[pl.ds(pick * half, half)]
        sources = [
            (away == 2, over_ref),
            (away == 4, far_ref),
            (((away == 1) & jnp.logical_not(second)) | ((away == 3) & second), over_twin_ref),
            ((away == 3) & jnp.logical_not(second), far_twin_ref),
            ((away == 1) & second, own_twin_ref.at[pl.ds(shared, half)]),
        ]
        for flag, source in sources:

            @pl.when(flag)
            def _():
                pltpu.make_async_copy(source, target, sems.at[pick]).start()

        copies.append(pltpu.make_async_copy(over_ref, target, sems.at[pick]))
    step = hidden // 2
    weight_copies = []
    for part in range(2 * hidden // step):
        copy = pltpu.make_async_copy(
            w_ref.at[:, pl.ds(2 * hidden + part * step, step)],
            w_buf.at[:, pl.ds(part * step, step)],
            sems.at[picks + part],
        )
        copy.start()
        weight_copies.append(copy)
    if last:
        out_copy = pltpu.make_async_copy(w_out_ref, out_buf, sems.at[picks + 2 * hidden // step])
        out_copy.start()
    acc_ref[...] = before_ref[...]
    for copy in copies:
        copy.wait()
    normed = centered(rows_ref[...].astype(F32)).astype(BF16)
    for part, copy in enumerate(weight_copies):
        copy.wait()
        columns = pl.ds(part * step, step)
        value = jnp.dot(normed, w_buf[:, columns], preferred_element_type=F32)
        pair_ref[:, columns] = silu_of_half(0.5 * value).astype(BF16)

    base = time_base(me, count, rows)
    first_start = starts_of(base, lengths_ref)
    gap = iota((LANES, LANES), 0) - iota((LANES, LANES), 1)
    width = 4 * head_size
    scaled = head_rows(head_size, width, 0.5 * head_size**-0.5)
    chosen = head_rows(head_size, width, 1.0)
    q_tiles, k_tiles = rows // LANES, half // LANES
    shift = chunk * k_tiles

    @pl.loop(0, picks)
    def _(pick):
        away = lists_ref[0, pick]
        block = lax.rem(me - away + count, count)
        block_base = time_base(block, count, rows)
        key_base = block_base + shared
        useful = (block_base < base) & (key_base + half - 1 >= first_start)

        @pl.when(useful)
        def _():
            start = starts_of(base + iota((rows, LANES), 0), lengths_ref)
            for tile in range(k_tiles):
                key_time = key_base + tile * LANES + iota((rows, LANES), 1)
                mask_ref[:, tile * LANES : (tile + 1) * LANES] = jnp.where(
                    key_time >= start, 0.0, BLOCKED
                )
            lows, highs = {}, {}
            for diff in range(-(shift + k_tiles - 1), q_tiles - shift):
                delta = away * rows + diff * LANES
                bucket, power = jnp.int32(8), jnp.int32(0)
                for degree in range(8, rel_ref.shape[1] - 1):
                    bucket = bucket + (delta >= 2**degree).astype(jnp.int32)
                    power = power + (delta == 2**degree).astype(jnp.int32)
                highs[diff] = bucket
                lows[diff] = bucket - power
            special = 1 - q_tiles
            if special in highs:

                @pl.when(away == 1)
                def _():
                    @pl.loop(0, head_count)
                    def _(head):
                        near_ref[head] = bias_chain(gap + LANES, rel_ref, head, 1, 1, 8)

                @pl.when(away != 1)
                def _():
                    @pl.loop(0, head_count)
                    def _(head):
                        near_ref[head] = jnp.full(
                            gap.shape, half_bias(rel_ref, head, highs[special]), F32
                        )

            key_rows = pl.ds(pl.multiple_of(pick * half, half), half)
            for group in range(hidden // width):
                columns = slice(group * width, (group + 1) * width)
                queries = q_ref[:, columns]
                values = pair_ref[key_rows, columns]
                keys = pair_ref[key_rows, hidden + group * width : hidden + (group + 1) * width]
                weights, stacked = [], []
                for num in range(width // head_size):
                    head = group * (width // head_size) + num
                    scores = lax.dot_general(
                        queries * scaled[num], keys, NT, preferred_element_type=F32
                    )
                    lines = []
                    for q_tile in range(q_tiles):
                        line = []
                        for k_tile in range(k_tiles):
                            diff = q_tile - k_tile - shift
                            if diff == special:
                                bias = near_ref[head]
                            elif diff in (0, 2 - q_tiles):
                                bias = jnp.where(
                                    gap >= 0,
                                    half_bias(rel_ref, head, highs[diff]),
                                    half_bias(rel_ref, head, lows[diff]),
                                )
                            else:
                                bias = half_bias(rel_ref, head, highs[diff])
                            spot = (
                                slice(q_tile * LANES, (q_tile + 1) * LANES),
                                slice(k_tile * LANES, (k_tile + 1) * LANES),
                            )
                            line.append(
                                silu_of_half(scores[spot] + bias + mask_ref[spot]).astype(BF16)
                            )
                        lines.append(jnp.concatenate(line, 1))
                    weights.append(jnp.concatenate(lines, 0))
                    stacked.append(values * chosen[num])
                acc_ref[:, columns] += jnp.dot(
                    jnp.concatenate(weights, 1),
                    jnp.concatenate(stacked, 0),
                    preferred_element_type=F32,
                )

    if not last:
        return
    wanted = cand_ref.shape[1]
    own = jnp.broadcast_to(cand_ref[pl.ds(me, 1), :].astype(F32), (wanted, wanted))
    diagonal = iota((wanted, wanted), 0) == iota((wanted, wanted), 1)
    own_column = jnp.sum(jnp.where(diagonal, own, 0.0), 1, keepdims=True)
    owner = jnp.floor(own * (1.0 / rows))
    owner_column = jnp.floor(own_column * (1.0 / rows))
    before = iota((wanted, wanted), 1) < iota((wanted, wanted), 0)
    rank = jnp.sum(jnp.where((owner == owner_column) & before, 1.0, 0.0), 1, keepdims=True)
    slot = (owner_column * slot_cap + rank).astype(jnp.int32)
    hits = (slot == iota((wanted, flat_ref.shape[0]), 1)).astype(BF16)
    listed = jnp.dot(hits, flat_ref[...], preferred_element_type=F32).astype(BF16)
    out_copy.wait()
    scale = hidden**-0.5
    total = count * rows
    for part in range(2):
        block_rows = slice(part * half, (part + 1) * half)
        gated = centered(acc_ref[block_rows]) * gate_ref[block_rows].astype(F32)
        layer = events_ref[block_rows].astype(F32) + jnp.dot(
            gated.astype(BF16), out_buf[...], preferred_element_type=F32
        )
        layer = layer.astype(BF16)
        layer_ref[block_rows] = layer
        table_ref[block_rows] = (
            lax.dot_general(layer, listed, NT, preferred_element_type=F32) * scale
        )
        following = pltpu.roll(events_ref[block_rows].astype(F32), half - 1, 0)
        if part == 0:
            after = events_ref[half : half + 16][:1].astype(F32)
        else:
            after = next_ref[...][:1].astype(F32)
        following = jnp.where(iota((half, hidden), 0) == half - 1, after, following)
        inner = jnp.sum(layer.astype(F32) * following, 1, keepdims=True) * scale
        for tile in range(half // LANES):
            spot = inner[tile * LANES : (tile + 1) * LANES]
            line = jnp.sum(jnp.where(diagonal, spot, 0.0), 0, keepdims=True)
            offset = part * half + tile * LANES
            coming = base + offset + 1 + iota((1, LANES), 1)
            same = coming < total
            end = jnp.int32(0)
            for user in range(lengths_ref.shape[0]):
                end = end + lengths_ref[user]
                same = same & (coming != end)
            score_ref[offset // LANES : offset // LANES + 1] = jnp.where(same, line, 0.0)


def smem():
    return pl.BlockSpec(memory_space=pltpu.SMEM)


def vmem():
    return pl.BlockSpec(memory_space=pltpu.VMEM)


def anywhere():
    return pl.BlockSpec(memory_space=pl.ANY)


def params(*semantics):
    return pltpu.CompilerParams(
        dimension_semantics=semantics or None, vmem_limit_bytes=VMEM_BYTES
    )


def shards(events, w_in, w_out, rel_bias, lengths, block_lists, candidates):
    rows, hidden = events.shape
    head_count = rel_bias.shape[0]
    head_size = hidden // head_count
    count = lax.axis_size("ctx")
    me = lax.axis_index("ctx")
    wanted = candidates.shape[1]
    slot_cap = 2 * wanted // count
    slots = count * slot_cap
    half = rows // 2
    width = 4 * head_size
    picks = block_lists.shape[1]

    onward = [(s, (s + 4) % count) for s in range(count)]
    across = [(s, s ^ 2) for s in range(count)]
    twin = [(s, s ^ 1) for s in range(count)]
    back = [(s, (s - 1) % count) for s in range(count)]

    halves = [events[:half], events[half:]]
    far = [passed_along(h, onward) for h in halves]
    own_twin = passed_along(events, twin)
    next_first = passed_along(events[:1], back)

    fetched = pl.pallas_call(
        functools.partial(request_kernel, slot_cap),
        out_shape=jax.ShapeDtypeStruct((slots, hidden), BF16),
        in_specs=[vmem(), vmem()],
        out_specs=vmem(),
        compiler_params=params(),
        cost_estimate=pl.CostEstimate(flops=10**9, bytes_accessed=2**21, transcendentals=0),
        name="request",
    )(candidates, events)

    step = hidden // 2
    projected = pl.pallas_call(
        project_kernel,
        grid=(4 * hidden // step,),
        out_shape=jax.ShapeDtypeStruct((rows, 4 * hidden), BF16),
        in_specs=[
            pl.BlockSpec((rows, hidden), lambda i: (0, 0)),
            pl.BlockSpec((hidden, step), lambda i: (0, i)),
        ],
        out_specs=pl.BlockSpec((rows, step), lambda i: (0, i)),
        scratch_shapes=[pltpu.VMEM((rows, hidden), BF16)],
        compiler_params=params("arbitrary"),
        cost_estimate=pl.CostEstimate(flops=7 * 10**9, bytes_accessed=2**23, transcendentals=0),
        name="project",
    )(events, w_in)

    groups = hidden // width

    def columns(which):
        return pl.BlockSpec((rows, width), lambda i: (0, which * groups + i))

    attended = pl.pallas_call(
        functools.partial(own_kernel, head_size),
        grid=(groups,),
        out_shape=jax.ShapeDtypeStruct((rows, hidden), F32),
        in_specs=[smem(), smem(), columns(1), columns(2), columns(3)],
        out_specs=pl.BlockSpec((rows, width), lambda i: (0, i)),
        scratch_shapes=[pltpu.VMEM((rows, rows), F32)],
        compiler_params=params("arbitrary"),
        cost_estimate=pl.CostEstimate(flops=6 * 10**9, bytes_accessed=2**22, transcendentals=0),
        name="own",
    )(lengths, rel_bias, projected, projected, projected)

    lower = (me // 2) % 2 == 0
    over = [
        passed_along(jnp.where(lower, halves[i], far[i]), across) for i in range(2)
    ]
    far_twin = [passed_along(f, twin) for f in far]
    over_twin = [passed_along(o, twin) for o in over]
    fetched, _ = lax.optimization_barrier((fetched, far[1]))
    arrived = lax.all_to_all(
        fetched.reshape(count, slot_cap, hidden), "ctx", split_axis=0, concat_axis=0, tiled=True
    ).reshape(slots, hidden)

    def column_block(which):
        return pl.BlockSpec((rows, hidden), lambda i: (0, which))

    whole = lambda *shape: pl.BlockSpec(shape, lambda i: (0,) * len(shape))
    parts = 2 * hidden // step
    for i in range(2):
        last = i == 1
        in_specs = [smem(), smem(), smem(), column_block(1), whole(rows, hidden)]
        in_specs += [anywhere()] * 6
        operands = [lengths, block_lists, rel_bias, projected, attended]
        operands += [over[i], far[i], over_twin[i], far_twin[i], own_twin, w_in]
        scratch = [
            pltpu.VMEM((picks * half, hidden), BF16),
            pltpu.VMEM((hidden, 2 * hidden), BF16),
            pltpu.VMEM((picks * half, 2 * hidden), BF16),
            pltpu.VMEM((rows, half), F32),
            pltpu.VMEM((head_count, LANES, LANES), F32),
            pltpu.SemaphoreType.DMA((picks + parts + 1,)),
        ]
        if last:
            in_specs += [
                column_block(0),
                whole(rows, hidden),
                whole(1, hidden),
                whole(slots, hidden),
                whole(count, wanted),
                anywhere(),
            ]
            operands += [projected, events, next_first, arrived, candidates, w_out]
            out_shape = (
                jax.ShapeDtypeStruct((rows, hidden), BF16),
                jax.ShapeDtypeStruct((rows // LANES, LANES), F32),
                jax.ShapeDtypeStruct((rows, wanted), F32),
            )
            out_specs = (
                whole(rows, hidden),
                whole(rows // LANES, LANES),
                whole(rows, wanted),
            )
            scratch = (
                [pltpu.VMEM((rows, hidden), F32)]
                + scratch
                + [pltpu.VMEM((hidden, hidden), BF16)]
            )
        else:
            out_shape = jax.ShapeDtypeStruct((rows, hidden), F32)
            out_specs = whole(rows, hidden)
        attended = pl.pallas_call(
            functools.partial(picks_kernel, i, last, head_size, slot_cap),
            grid=(1,),
            out_shape=out_shape,
            in_specs=in_specs,
            out_specs=out_specs,
            scratch_shapes=scratch,
            compiler_params=params("arbitrary"),
            cost_estimate=pl.CostEstimate(
                flops=8 * 10**9, bytes_accessed=2**22, transcendentals=0
            ),
            name="last_picks" if last else "first_picks",
        )(*operands)
    layer_output, next_score, table = attended
    return (layer_output, next_score.reshape(rows), table)


def solution(mesh):
    in_specs = (
        P(("groups", "ctx"), None),
        P(),
        P(),
        P(),
        P("groups"),
        P(("groups", "ctx"), None),
        P("groups", None),
    )
    out_specs = (P(("groups", "ctx"), None), P(("groups", "ctx")), P(("groups", "ctx"), None))
    return jax.shard_map(shards, mesh=mesh, in_specs=in_specs, out_specs=out_specs, check_vma=False)
```

```python
import functools

import jax
import jax.numpy as jnp
from jax import lax
from jax.experimental import pallas as pl
from jax.experimental.pallas import tpu as pltpu
from jax.sharding import PartitionSpec as P

BLOCKED = -1e9
LANES = 128
F32 = jnp.float32
BF16 = jnp.bfloat16
NT = (((1,), (1,)), ((), ()))


def passed_along(value, pairs):
    return lax.ppermute(value, "ctx", pairs)


def centered(values):
    center = values - jnp.mean(values, -1, keepdims=True)
    spread = jnp.mean(center * center, -1, keepdims=True)
    return center * lax.rsqrt(spread + 1e-05)


def silu_of_half(half):
    return half * jnp.tanh(half) + half


def iota(shape, dim):
    return lax.broadcasted_iota(jnp.int32, shape, dim)


def time_base(block, count, rows):
    total = count * rows
    return lax.rem(block * rows + total // 4, total)


def starts_of(times, lengths_ref):
    end = jnp.int32(0)
    start = jnp.zeros_like(times)
    for user in range(lengths_ref.shape[0]):
        length = lengths_ref[user]
        end = end + length
        start = start + jnp.where(times >= end, length, 0)
    return start


def half_bias(rel_ref, head, bucket):
    return rel_ref[head, bucket] * 0.5


def bias_chain(distance, rel_ref, head, low, first, last):
    tile = jnp.full(distance.shape, half_bias(rel_ref, head, low), F32)
    for degree in range(first, last):
        tile = jnp.where(distance >= 2**degree, half_bias(rel_ref, head, degree + 1), tile)
    return tile


def head_rows(size, width, value):
    lane = iota((1, width), 1)
    return [
        jnp.where((lane >= size * num) & (lane < size * (num + 1)), value, 0.0).astype(BF16)
        for num in range(width // size)
    ]


def requested_rows(slot_cap, cand_ref, events):
    me = lax.axis_index("ctx")
    count, wanted = cand_ref.shape
    rows = events.shape[0]
    slots = count * slot_cap
    cand = cand_ref[...]
    local = cand - me * rows
    mine = (local >= 0) & (local < rows)
    earlier = (iota((wanted, wanted), 0) < iota((wanted, wanted), 1)).astype(BF16)
    rank = jnp.dot(jnp.where(mine, 1.0, 0.0).astype(BF16), earlier, preferred_element_type=F32)
    code = jnp.where(mine, rank * rows + local.astype(F32), -1.0)
    slot_num = iota((slots, count), 0) - iota((slots, count), 1) * slot_cap
    spread = jnp.where((slot_num >= 0) & (slot_num < slot_cap), 1.0, 0.0)
    asked = jnp.dot(spread, code, preferred_element_type=F32, precision=lax.Precision.HIGHEST)
    slot = lax.rem(iota((slots, wanted), 0), slot_cap).astype(F32)
    found = asked - slot * rows
    ids = jnp.sum(jnp.where((found >= 0.0) & (found < rows), found + 1.0, 0.0), 1, keepdims=True)
    picks = (ids.astype(jnp.int32) - 1 == iota((slots, rows), 1)).astype(BF16)
    return jnp.dot(picks, events, preferred_element_type=F32).astype(BF16)


def request_kernel(slot_cap, cand_ref, events_ref, sent_ref):
    sent_ref[...] = requested_rows(slot_cap, cand_ref, events_ref[...])


def front_kernel(events_hbm, w_ref, out_ref, bottom_ref, *scratch):
    events_ref, w_buf, out_buf, in_sems, out_sems = scratch
    arrival = pltpu.make_async_copy(events_hbm, events_ref, in_sems.at[4])
    arrival.start()
    hidden = events_ref.shape[1]
    piece = hidden // 4
    order = [1, 3, 2, 0]
    columns = [pl.ds(part * hidden, hidden) for part in range(len(order))]
    arrivals = [
        pltpu.make_async_copy(w_ref.at[:, spot], w_buf.at[:, spot], in_sems.at[part])
        for part, spot in enumerate(columns)
    ]
    leaving = [
        pltpu.make_async_copy(out_buf.at[:, spot], out_ref.at[:, spot], out_sems.at[part])
        for part, spot in enumerate(columns)
    ]
    for part in order:
        arrivals[part].start()
    half = bottom_ref.shape[0]
    bottom = pltpu.make_async_copy(events_ref.at[pl.ds(half, half)], bottom_ref, out_sems.at[4])
    arrival.wait()
    bottom.start()
    normed = centered(events_ref[...].astype(F32)).astype(BF16)
    for part in order:
        arrivals[part].wait()
        for start in range(part * hidden, (part + 1) * hidden, piece):
            spot = slice(start, start + piece)
            value = jnp.dot(normed, w_buf[:, spot], preferred_element_type=F32)
            out_buf[:, spot] = silu_of_half(0.5 * value).astype(BF16)
        leaving[part].start()
    for part in order:
        leaving[part].wait()
    bottom.wait()


def own_kernel(head_size, lengths_ref, rel_ref, q_ref, v_ref, k_ref, out_ref, mask_ref):
    group = pl.program_id(0)
    rows, width = q_ref.shape
    half = rows // 2
    heads = width // head_size
    count = lax.axis_size("ctx")

    @pl.when(group == 0)
    def _():
        base = time_base(lax.axis_index("ctx"), count, rows)
        start = starts_of(base + iota((rows, LANES), 0), lengths_ref)
        for num in range(rows // LANES):
            key_time = base + num * LANES + iota((rows, LANES), 1)
            mask_ref[:, num * LANES : (num + 1) * LANES] = jnp.where(key_time >= start, 0.0, BLOCKED)

    away = iota((LANES, LANES), 0) - iota((LANES, LANES), 1)
    queries, values, keys = q_ref[...], v_ref[...], k_ref[...]
    scaled = head_rows(head_size, width, 0.5 * head_size**-0.5)
    chosen = head_rows(head_size, width, 1.0)
    parts = [([], []), ([], [])]
    for num in range(heads):
        head = group * heads + num
        tiles = [
            jnp.where(away < 0, BLOCKED, bias_chain(away, rel_ref, head, 0, 0, 7)),
            bias_chain(away + LANES, rel_ref, head, 1, 1, 8),
            jnp.where(away >= 0, half_bias(rel_ref, head, 9), half_bias(rel_ref, head, 8)),
            half_bias(rel_ref, head, 9),
        ]
        head_queries = queries * scaled[num]
        head_values = values * chosen[num]
        for part in range(2):
            seen = (part + 1) * half
            scores = lax.dot_general(
                head_queries[part * half : (part + 1) * half],
                keys[:seen],
                NT,
                preferred_element_type=F32,
            )
            lines = []
            for q_sub in range(half // LANES):
                q_tile = part * (half // LANES) + q_sub
                line = []
                for k_tile in range(seen // LANES):
                    if k_tile > q_tile:
                        line.append(jnp.zeros((LANES, LANES), BF16))
                        continue
                    part_scores = scores[
                        q_sub * LANES : (q_sub + 1) * LANES, k_tile * LANES : (k_tile + 1) * LANES
                    ]
                    mask = mask_ref[
                        q_tile * LANES : (q_tile + 1) * LANES, k_tile * LANES : (k_tile + 1) * LANES
                    ]
                    line.append(
                        silu_of_half(part_scores + tiles[q_tile - k_tile] + mask).astype(BF16)
                    )
                lines.append(jnp.concatenate(line, 1))
            parts[part][0].append(jnp.concatenate(lines, 0))
            parts[part][1].append(head_values[:seen])
    for part in range(2):
        weights = jnp.concatenate(parts[part][0], 1)
        stacked = jnp.concatenate(parts[part][1], 0)
        out_ref[part * half : (part + 1) * half] = jnp.dot(
            weights, stacked, preferred_element_type=F32
        )


def picks_kernel(head_size, *refs):
    lengths_ref, lists_ref, rel_ref, projected_ref, before_ref = refs[:5]
    far_ref, far_twin_ref, own_twin_ref, across_ref, across_twin_ref = refs[5:10]
    passed_ref, passed_twin_ref, over_ref, over_twin_ref, w_ref = refs[10:15]
    events_hbm, next_ref, w_out_ref = refs[15:18]
    layer_hbm, score_ref = refs[18:20]
    acc_ref, q_ref, earlier_ref, rows_ref, w_buf, pair_ref, mask_ref, near_ref = refs[20:28]
    sems, out_buf, gate_ref, events_ref, layer_ref, layer_sems = refs[28:]
    me = lax.axis_index("ctx")
    count = lax.axis_size("ctx")
    rows, hidden = q_ref.shape
    half = rows // 2
    picks = lists_ref.shape[1]
    head_count, _ = rel_ref.shape
    second = lax.rem(me, 2) == 1
    first = jnp.logical_not(second)
    upper = lax.rem(me, 4) >= 2
    lower = jnp.logical_not(upper)

    copies = []
    for pick in range(picks):
        away = lists_ref[0, pick]
        crossed = ((away == 1) & first) | ((away == 3) & second)
        target = rows_ref.at[pl.ds(pick * rows, rows)]
        head = rows_ref.at[pl.ds(pick * rows, half)]
        tail = rows_ref.at[pl.ds(pick * rows + half, half)]
        sources = [
            (away == 4, far_ref, target),
            ((away == 3) & first, far_twin_ref, target),
            ((away == 1) & second, own_twin_ref, target),
            ((away == 2) & upper, across_ref, head),
            ((away == 2) & lower, passed_ref, head),
            (away == 2, over_ref, tail),
            (crossed & upper, across_twin_ref, head),
            (crossed & lower, passed_twin_ref, head),
            (crossed, over_twin_ref, tail),
        ]
        for flag, source, spot in sources:

            @pl.when(flag)
            def _():
                pltpu.make_async_copy(source, spot, sems.at[pick]).start()

        copies.append(pltpu.make_async_copy(far_ref, target, sems.at[pick]))
    step = hidden // 2
    parts = 2 * hidden // step
    later = [
        (w_ref.at[:, pl.ds(2 * hidden + part * step, step)], w_buf.at[:, pl.ds(part * step, step)])
        for part in range(parts)
    ]
    later.append((projected_ref.at[:, pl.ds(hidden, hidden)], q_ref))
    later.append((before_ref, earlier_ref))
    later.append((w_out_ref, out_buf))
    later.append((projected_ref.at[:, pl.ds(0, hidden)], gate_ref))
    later.append((events_hbm, events_ref))
    later = [
        pltpu.make_async_copy(source, target, sems.at[picks + num])
        for num, (source, target) in enumerate(later)
    ]
    for copy in later[:parts]:
        copy.start()
    acc_ref[...] = jnp.zeros_like(acc_ref)
    for copy in copies:
        copy.wait()
    normed = centered(rows_ref[...].astype(F32)).astype(BF16)
    for part in range(parts):
        later[part].wait()
        if part == 0:
            for copy in later[parts:]:
                copy.start()
        columns = pl.ds(part * step, step)
        value = jnp.dot(normed, w_buf[:, columns], preferred_element_type=F32)
        pair_ref[:, columns] = silu_of_half(0.5 * value).astype(BF16)
    later[parts].wait()

    base = time_base(me, count, rows)
    first_start = starts_of(base, lengths_ref)
    gap = iota((LANES, LANES), 0) - iota((LANES, LANES), 1)
    width = 4 * head_size
    scaled = head_rows(head_size, width, 0.5 * head_size**-0.5)
    chosen = head_rows(head_size, width, 1.0)
    tiles = rows // LANES

    @pl.loop(0, picks)
    def _(pick):
        away = lists_ref[0, pick]
        block = lax.rem(me - away + count, count)
        key_base = time_base(block, count, rows)
        useful = (key_base < base) & (key_base + rows - 1 >= first_start)

        @pl.when(useful)
        def _():
            start = starts_of(base + iota((rows, LANES), 0), lengths_ref)
            for tile in range(tiles):
                key_time = key_base + tile * LANES + iota((rows, LANES), 1)
                mask_ref[:, tile * LANES : (tile + 1) * LANES] = jnp.where(
                    key_time >= start, 0.0, BLOCKED
                )
            lows, highs = {}, {}
            for diff in range(1 - tiles, tiles):
                delta = away * rows + diff * LANES
                bucket, power = jnp.int32(8), jnp.int32(0)
                for degree in range(8, rel_ref.shape[1] - 1):
                    bucket = bucket + (delta >= 2**degree).astype(jnp.int32)
                    power = power + (delta == 2**degree).astype(jnp.int32)
                highs[diff] = bucket
                lows[diff] = bucket - power
            special = 1 - tiles

            @pl.when(away == 1)
            def _():
                @pl.loop(0, head_count)
                def _(head):
                    near_ref[head] = bias_chain(gap + LANES, rel_ref, head, 1, 1, 8)

            @pl.when(away != 1)
            def _():
                @pl.loop(0, head_count)
                def _(head):
                    near_ref[head] = jnp.full(
                        gap.shape, half_bias(rel_ref, head, highs[special]), F32
                    )

            key_rows = pl.ds(pl.multiple_of(pick * rows, rows), rows)
            for group in range(hidden // width):
                columns = slice(group * width, (group + 1) * width)
                queries = q_ref[:, columns]
                values = pair_ref[key_rows, columns]
                keys = pair_ref[key_rows, hidden + group * width : hidden + (group + 1) * width]
                weights, stacked = [], []
                for num in range(width // head_size):
                    head = group * (width // head_size) + num
                    scores = lax.dot_general(
                        queries * scaled[num], keys, NT, preferred_element_type=F32
                    )
                    lines = []
                    for q_tile in range(tiles):
                        line = []
                        for k_tile in range(tiles):
                            diff = q_tile - k_tile
                            if diff == special:
                                bias = near_ref[head]
                            elif diff in (0, 2 - tiles):
                                bias = jnp.where(
                                    gap >= 0,
                                    half_bias(rel_ref, head, highs[diff]),
                                    half_bias(rel_ref, head, lows[diff]),
                                )
                            else:
                                bias = half_bias(rel_ref, head, highs[diff])
                            spot = (
                                slice(q_tile * LANES, (q_tile + 1) * LANES),
                                slice(k_tile * LANES, (k_tile + 1) * LANES),
                            )
                            line.append(
                                silu_of_half(scores[spot] + bias + mask_ref[spot]).astype(BF16)
                            )
                        lines.append(jnp.concatenate(line, 1))
                    weights.append(jnp.concatenate(lines, 0))
                    stacked.append(values * chosen[num])
                acc_ref[:, columns] += jnp.dot(
                    jnp.concatenate(weights, 1),
                    jnp.concatenate(stacked, 0),
                    preferred_element_type=F32,
                )

    later[parts + 1].wait()
    diagonal = iota((LANES, LANES), 0) == iota((LANES, LANES), 1)
    for copy in later[parts + 2 :]:
        copy.wait()
    scale = hidden**-0.5
    total = count * rows
    departures = []
    for part in range(2):
        block_rows = slice(part * half, (part + 1) * half)
        attended = acc_ref[block_rows] + earlier_ref[block_rows]
        gated = centered(attended) * gate_ref[block_rows].astype(F32)
        layer = events_ref[block_rows].astype(F32) + jnp.dot(
            gated.astype(BF16), out_buf[...], preferred_element_type=F32
        )
        layer = layer.astype(BF16)
        layer_ref[block_rows] = layer
        leaving = pltpu.make_async_copy(
            layer_ref.at[pl.ds(part * half, half)],
            layer_hbm.at[pl.ds(part * half, half)],
            layer_sems.at[part],
        )
        leaving.start()
        departures.append(leaving)
        following = pltpu.roll(events_ref[block_rows].astype(F32), half - 1, 0)
        if part == 0:
            after = events_ref[half : half + 16][:1].astype(F32)
        else:
            after = next_ref[...].astype(F32)
        following = jnp.where(iota((half, hidden), 0) == half - 1, after, following)
        inner = jnp.sum(layer.astype(F32) * following, 1, keepdims=True) * scale
        for tile in range(half // LANES):
            spot = inner[tile * LANES : (tile + 1) * LANES]
            line = jnp.sum(jnp.where(diagonal, spot, 0.0), 0, keepdims=True)
            offset = part * half + tile * LANES
            coming = base + offset + 1 + iota((1, LANES), 1)
            same = coming < total
            end = jnp.int32(0)
            for user in range(lengths_ref.shape[0]):
                end = end + lengths_ref[user]
                same = same & (coming != end)
            score_ref[offset // LANES : offset // LANES + 1] = jnp.where(same, line, 0.0)
    for leaving in departures:
        leaving.wait()


def table_kernel(slot_cap, layer_ref, flat_ref, cand_ref, table_ref):
    me = lax.axis_index("ctx")
    rows, hidden = layer_ref.shape
    wanted = cand_ref.shape[1]
    own = jnp.broadcast_to(cand_ref[pl.ds(me, 1), :].astype(F32), (wanted, wanted))
    diagonal = iota((wanted, wanted), 0) == iota((wanted, wanted), 1)
    own_column = jnp.sum(jnp.where(diagonal, own, 0.0), 1, keepdims=True)
    owner = jnp.floor(own * (1.0 / rows))
    owner_column = jnp.floor(own_column * (1.0 / rows))
    before = iota((wanted, wanted), 1) < iota((wanted, wanted), 0)
    rank = jnp.sum(jnp.where((owner == owner_column) & before, 1.0, 0.0), 1, keepdims=True)
    slot = (owner_column * slot_cap + rank).astype(jnp.int32)
    hits = (slot == iota((wanted, flat_ref.shape[0]), 1)).astype(BF16)
    listed = jnp.dot(hits, flat_ref[...], preferred_element_type=F32).astype(BF16)
    scores = lax.dot_general(layer_ref[...], listed, NT, preferred_element_type=F32)
    table_ref[...] = scores * hidden**-0.5


def smem():
    return pl.BlockSpec(memory_space=pltpu.SMEM)


def vmem():
    return pl.BlockSpec(memory_space=pltpu.VMEM)


def hbm():
    return pl.BlockSpec(memory_space=pltpu.HBM)


def anywhere():
    return pl.BlockSpec(memory_space=pl.ANY)


def placed(value):
    return pltpu.with_memory_space_constraint(value, pltpu.HBM)


def params(mebibytes, *semantics):
    return pltpu.CompilerParams(
        dimension_semantics=semantics or None, vmem_limit_bytes=mebibytes * 2**20
    )


def shards(events, w_in, w_out, rel_bias, lengths, block_lists, candidates):
    rows, hidden = events.shape
    head_count = rel_bias.shape[0]
    head_size = hidden // head_count
    count = lax.axis_size("ctx")
    wanted = candidates.shape[1]
    slot_cap = 2 * wanted // count
    slots = count * slot_cap
    half = rows // 2
    width = 4 * head_size
    picks = block_lists.shape[1]

    ring = range(count)
    across_pairs = [(s, s ^ 2) for s in ring]
    over_pairs = [(s, (s + 2) % count) for s in ring]
    far_pairs = [(s, (s + 4) % count) for s in ring]
    passing_pairs = [(s, (s + 4) % count) for s in ring if s % 4 < 2]
    back_pairs = [(s, (s - 1) % count) for s in ring]
    up_pairs = [(s, s + 1) for s in ring if s % 2 == 0]
    down_pairs = [(s, s - 1) for s in ring if s % 2 == 1]
    twin_pairs = [(s, s ^ 1) for s in ring]
    upper_twins = [(s, s ^ 1) for s in ring if s % 4 >= 2]
    lower_twins = [(s, s ^ 1) for s in ring if s % 4 < 2]

    next_first = passed_along(events[:1], back_pairs)
    own_twin = passed_along(events, up_pairs)
    across = passed_along(events[:half], across_pairs)
    far = passed_along(events, far_pairs)

    projected, bottom = pl.pallas_call(
        front_kernel,
        out_shape=(pltpu.HBM((rows, 4 * hidden), BF16), pltpu.HBM((half, hidden), BF16)),
        in_specs=[hbm(), hbm()],
        out_specs=(hbm(), hbm()),
        scratch_shapes=[
            pltpu.VMEM((rows, hidden), BF16),
            pltpu.VMEM((hidden, 4 * hidden), BF16),
            pltpu.VMEM((rows, 4 * hidden), BF16),
            pltpu.SemaphoreType.DMA((5,)),
            pltpu.SemaphoreType.DMA((5,)),
        ],
        compiler_params=params(30),
        cost_estimate=pl.CostEstimate(flops=8 * 10**9, bytes_accessed=2**23, transcendentals=0),
        name="front",
    )(placed(events), placed(w_in))

    across, projected = lax.optimization_barrier((across, projected))
    passed = passed_along(across, passing_pairs)
    over = passed_along(bottom, over_pairs)
    groups = hidden // width

    def columns(which):
        return pl.BlockSpec((rows, width), lambda i: (0, which * groups + i))

    attended = pl.pallas_call(
        functools.partial(own_kernel, head_size),
        grid=(groups,),
        out_shape=pltpu.HBM((rows, hidden), F32),
        in_specs=[smem(), smem(), columns(1), columns(2), columns(3)],
        out_specs=pl.BlockSpec((rows, width), lambda i: (0, i)),
        scratch_shapes=[pltpu.VMEM((rows, rows), F32)],
        compiler_params=params(16, "arbitrary"),
        cost_estimate=pl.CostEstimate(flops=6 * 10**9, bytes_accessed=2**22, transcendentals=0),
        name="own",
    )(lengths, rel_bias, *[placed(projected)] * 3)

    across, far, whole, _ = lax.optimization_barrier((across, far, events, attended))
    fetched = pl.pallas_call(
        functools.partial(request_kernel, slot_cap),
        out_shape=jax.ShapeDtypeStruct((slots, hidden), BF16),
        in_specs=[vmem(), vmem()],
        out_specs=vmem(),
        compiler_params=params(10),
        cost_estimate=pl.CostEstimate(flops=10**9, bytes_accessed=2**21, transcendentals=0),
        name="request",
    )(candidates, whole)
    over, passed, _ = lax.optimization_barrier((over, passed, fetched))
    across_twin = passed_along(across, upper_twins)
    over_twin = passed_along(over, twin_pairs)
    far_twin = passed_along(far, down_pairs)
    passed_twin = passed_along(passed, lower_twins)
    arrived = lax.all_to_all(
        fetched.reshape(count, slot_cap, hidden), "ctx", split_axis=0, concat_axis=0, tiled=True
    ).reshape(slots, hidden)

    parts = 4
    operands = [placed(projected), placed(attended), far, far_twin, own_twin, across]
    operands += [across_twin, passed, passed_twin, over, over_twin, placed(w_in), placed(events)]
    layer_output, next_score = pl.pallas_call(
        functools.partial(picks_kernel, head_size),
        out_shape=(
            pltpu.HBM((rows, hidden), BF16),
            jax.ShapeDtypeStruct((rows // LANES, LANES), F32),
        ),
        in_specs=[smem()] * 3 + [hbm()] * 2 + [anywhere()] * 9 + [hbm()] * 2 + [vmem(), hbm()],
        out_specs=(hbm(), vmem()),
        scratch_shapes=[
            pltpu.VMEM((rows, hidden), F32),
            pltpu.VMEM((rows, hidden), BF16),
            pltpu.VMEM((rows, hidden), F32),
            pltpu.VMEM((picks * rows, hidden), BF16),
            pltpu.VMEM((hidden, 2 * hidden), BF16),
            pltpu.VMEM((picks * rows, 2 * hidden), BF16),
            pltpu.VMEM((rows, rows), F32),
            pltpu.VMEM((head_count, LANES, LANES), F32),
            pltpu.SemaphoreType.DMA((picks + parts + 5,)),
            pltpu.VMEM((hidden, hidden), BF16),
            pltpu.VMEM((rows, hidden), BF16),
            pltpu.VMEM((rows, hidden), BF16),
            pltpu.VMEM((rows, hidden), BF16),
            pltpu.SemaphoreType.DMA((2,)),
        ],
        compiler_params=params(50),
        cost_estimate=pl.CostEstimate(
            flops=20 * 10**9, bytes_accessed=2**23, transcendentals=0
        ),
        name="picks",
    )(lengths, block_lists, rel_bias, *operands, next_first, placed(w_out))
    table = pl.pallas_call(
        functools.partial(table_kernel, slot_cap),
        out_shape=jax.ShapeDtypeStruct((rows, wanted), F32),
        in_specs=[vmem()] * 3,
        out_specs=vmem(),
        compiler_params=params(10),
        cost_estimate=pl.CostEstimate(flops=10**9, bytes_accessed=2**21, transcendentals=0),
        name="table",
    )(layer_output, arrived, candidates)
    return (layer_output, next_score.reshape(rows), table)


def solution(mesh):
    in_specs = (
        P(("groups", "ctx"), None),
        P(),
        P(),
        P(),
        P("groups"),
        P(("groups", "ctx"), None),
        P("groups", None),
    )
    out_specs = (P(("groups", "ctx"), None), P(("groups", "ctx")), P(("groups", "ctx"), None))
    return jax.shard_map(shards, mesh=mesh, in_specs=in_specs, out_specs=out_specs, check_vma=False)
```

```python
import functools

import jax
import jax.numpy as jnp
from jax import lax
from jax.experimental import pallas as pl
from jax.experimental.pallas import tpu as pltpu
from jax.sharding import PartitionSpec as P

BLOCKED = -1e9
LANES = 128
F32 = jnp.float32
BF16 = jnp.bfloat16
NT = (((1,), (1,)), ((), ()))


def passed_along(value, pairs):
    return lax.ppermute(value, "ctx", pairs)


def centered(values):
    center = values - jnp.mean(values, -1, keepdims=True)
    spread = jnp.mean(center * center, -1, keepdims=True)
    return center * lax.rsqrt(spread + 1e-05)


def silu_of_half(half):
    return half * jnp.tanh(half) + half


def iota(shape, dim):
    return lax.broadcasted_iota(jnp.int32, shape, dim)


def time_base(block, count, rows):
    total = count * rows
    return lax.rem(block * rows + total // 4, total)


def starts_of(times, lengths_ref):
    end = jnp.int32(0)
    start = jnp.zeros_like(times)
    for user in range(lengths_ref.shape[0]):
        length = lengths_ref[user]
        end = end + length
        start = start + jnp.where(times >= end, length, 0)
    return start


def half_bias(rel_ref, head, bucket):
    return rel_ref[head, bucket] * 0.5


def bias_chain(distance, rel_ref, head, low, first, last):
    tile = jnp.full(distance.shape, half_bias(rel_ref, head, low), F32)
    for degree in range(first, last):
        tile = jnp.where(distance >= 2**degree, half_bias(rel_ref, head, degree + 1), tile)
    return tile


def head_rows(size, width, value):
    lane = iota((1, width), 1)
    return [
        jnp.where((lane >= size * num) & (lane < size * (num + 1)), value, 0.0).astype(BF16)
        for num in range(width // size)
    ]


def requested_rows(slot_cap, cand_ref, events):
    me = lax.axis_index("ctx")
    count, wanted = cand_ref.shape
    rows = events.shape[0]
    slots = count * slot_cap
    cand = cand_ref[...]
    local = cand - me * rows
    mine = (local >= 0) & (local < rows)
    earlier = (iota((wanted, wanted), 0) < iota((wanted, wanted), 1)).astype(BF16)
    rank = jnp.dot(jnp.where(mine, 1.0, 0.0).astype(BF16), earlier, preferred_element_type=F32)
    code = jnp.where(mine, rank * rows + local.astype(F32), -1.0)
    slot_num = iota((slots, count), 0) - iota((slots, count), 1) * slot_cap
    spread = jnp.where((slot_num >= 0) & (slot_num < slot_cap), 1.0, 0.0)
    asked = jnp.dot(spread, code, preferred_element_type=F32, precision=lax.Precision.HIGHEST)
    slot = lax.rem(iota((slots, wanted), 0), slot_cap).astype(F32)
    found = asked - slot * rows
    ids = jnp.sum(jnp.where((found >= 0.0) & (found < rows), found + 1.0, 0.0), 1, keepdims=True)
    picks = (ids.astype(jnp.int32) - 1 == iota((slots, rows), 1)).astype(BF16)
    return jnp.dot(picks, events, preferred_element_type=F32).astype(BF16)


def own_attention(head_size, lengths_ref, rel_ref, pair_buf, mask_ref, out_ref, finish):
    rows, hidden = out_ref.shape
    half = rows // 2
    width = 4 * head_size
    heads = width // head_size
    base = time_base(lax.axis_index("ctx"), lax.axis_size("ctx"), rows)
    start = starts_of(base + iota((rows, LANES), 0), lengths_ref)
    for num in range(rows // LANES):
        key_time = base + num * LANES + iota((rows, LANES), 1)
        mask_ref[:, num * LANES : (num + 1) * LANES] = jnp.where(key_time >= start, 0.0, BLOCKED)
    away = iota((LANES, LANES), 0) - iota((LANES, LANES), 1)
    scaled = head_rows(head_size, width, 0.5 * head_size**-0.5)
    chosen = head_rows(head_size, width, 1.0)
    for group in range(hidden // width):
        spot = slice(group * width, (group + 1) * width)
        queries, values, keys = [
            pair_buf[:, which * hidden + spot.start : which * hidden + spot.stop]
            for which in (1, 2, 3)
        ]
        parts = [([], []), ([], [])]
        for num in range(heads):
            head = group * heads + num
            tiles = [
                jnp.where(away < 0, BLOCKED, bias_chain(away, rel_ref, head, 0, 0, 7)),
                bias_chain(away + LANES, rel_ref, head, 1, 1, 8),
                jnp.where(away >= 0, half_bias(rel_ref, head, 9), half_bias(rel_ref, head, 8)),
                half_bias(rel_ref, head, 9),
            ]
            head_queries = queries * scaled[num]
            head_values = values * chosen[num]
            for part in range(2):
                seen = (part + 1) * half
                scores = lax.dot_general(
                    head_queries[part * half : (part + 1) * half],
                    keys[:seen],
                    NT,
                    preferred_element_type=F32,
                )
                lines = []
                for q_sub in range(half // LANES):
                    q_tile = part * (half // LANES) + q_sub
                    line = []
                    for k_tile in range(seen // LANES):
                        if k_tile > q_tile:
                            line.append(jnp.zeros((LANES, LANES), BF16))
                            continue
                        k_spot = slice(k_tile * LANES, (k_tile + 1) * LANES)
                        part_scores = scores[q_sub * LANES : (q_sub + 1) * LANES, k_spot]
                        mask = mask_ref[q_tile * LANES : (q_tile + 1) * LANES, k_spot]
                        line.append(
                            silu_of_half(part_scores + tiles[q_tile - k_tile] + mask).astype(BF16)
                        )
                    lines.append(jnp.concatenate(line, 1))
                parts[part][0].append(jnp.concatenate(lines, 0))
                parts[part][1].append(head_values[:seen])
        for part in range(2):
            out_ref[part * half : (part + 1) * half, spot] = jnp.dot(
                jnp.concatenate(parts[part][0], 1),
                jnp.concatenate(parts[part][1], 0),
                preferred_element_type=F32,
            )
    finish()


def front_kernel(head_size, slot_cap, *refs):
    lengths_ref, rel_ref, cand_ref, events_hbm, w_ref = refs[:5]
    sent_ref, kept_hbm, attended_hbm, bottom_hbm = refs[5:9]
    events_ref, w_buf, pair_buf, out_buf, mask_ref, in_sems, out_sems = refs[9:]
    rows, hidden = events_ref.shape
    half = rows // 2
    step = hidden // 2
    arrival = pltpu.make_async_copy(events_hbm, events_ref, in_sems.at[8])
    arrival.start()
    order = [2, 3, 6, 7, 4, 5, 0, 1]
    arrivals = [
        pltpu.make_async_copy(
            w_ref.at[:, pl.ds(part * step, step)],
            w_buf.at[:, pl.ds(part * step, step)],
            in_sems.at[part],
        )
        for part in order
    ]
    bottom = pltpu.make_async_copy(events_ref.at[pl.ds(half, half)], bottom_hbm, out_sems.at[0])
    kept = pltpu.make_async_copy(pair_buf.at[:, pl.ds(0, 2 * hidden)], kept_hbm, out_sems.at[1])
    attended = pltpu.make_async_copy(out_buf, attended_hbm, out_sems.at[2])
    ahead = 2
    for copy in arrivals[:ahead]:
        copy.start()
    arrival.wait()
    bottom.start()
    normed = centered(events_ref[...].astype(F32)).astype(BF16)
    for num, part in enumerate(order):
        arrivals[num].wait()
        if num + ahead < len(arrivals):
            arrivals[num + ahead].start()
        for start in range(part * step, (part + 1) * step, step // 2):
            spot = slice(start, start + step // 2)
            value = jnp.dot(normed, w_buf[:, spot], preferred_element_type=F32)
            pair_buf[:, spot] = silu_of_half(0.5 * value).astype(BF16)
    kept.start()
    sent_ref[...] = requested_rows(slot_cap, cand_ref, events_ref[...])
    own_attention(head_size, lengths_ref, rel_ref, pair_buf, mask_ref, out_buf, attended.start)
    for copy in (bottom, kept, attended):
        copy.wait()


def picks_kernel(head_size, *refs):
    lengths_ref, lists_ref, rel_ref, projected_ref, before_ref = refs[:5]
    far_ref, far_twin_ref, own_twin_ref, across_ref, across_twin_ref = refs[5:10]
    passed_ref, passed_twin_ref, over_ref, over_twin_ref, w_ref = refs[10:15]
    events_hbm, next_ref, w_out_ref = refs[15:18]
    layer_hbm, score_ref = refs[18:20]
    acc_ref, q_ref, earlier_ref, rows_ref, w_buf, pair_ref, mask_ref, near_ref = refs[20:28]
    sems, out_buf, gate_ref, events_ref, layer_ref, layer_sems = refs[28:]
    me = lax.axis_index("ctx")
    count = lax.axis_size("ctx")
    rows, hidden = q_ref.shape
    half = rows // 2
    picks = lists_ref.shape[1]
    head_count, _ = rel_ref.shape
    second = lax.rem(me, 2) == 1
    first = jnp.logical_not(second)
    upper = lax.rem(me, 4) >= 2
    lower = jnp.logical_not(upper)

    copies = []
    for pick in range(picks):
        away = lists_ref[0, pick]
        crossed = ((away == 1) & first) | ((away == 3) & second)
        target = rows_ref.at[pl.ds(pick * rows, rows)]
        head = rows_ref.at[pl.ds(pick * rows, half)]
        tail = rows_ref.at[pl.ds(pick * rows + half, half)]
        sources = [
            (away == 4, far_ref, target),
            ((away == 3) & first, far_twin_ref, target),
            ((away == 1) & second, own_twin_ref, target),
            ((away == 2) & upper, across_ref, head),
            ((away == 2) & lower, passed_ref, head),
            (away == 2, over_ref, tail),
            (crossed & upper, across_twin_ref, head),
            (crossed & lower, passed_twin_ref, head),
            (crossed, over_twin_ref, tail),
        ]
        for flag, source, spot in sources:

            @pl.when(flag)
            def _():
                pltpu.make_async_copy(source, spot, sems.at[pick]).start()

        copies.append(pltpu.make_async_copy(far_ref, target, sems.at[pick]))
    step = hidden // 2
    parts = 2 * hidden // step
    later = [
        (w_ref.at[:, pl.ds(2 * hidden + part * step, step)], w_buf.at[:, pl.ds(part * step, step)])
        for part in range(parts)
    ]
    later.append((projected_ref.at[:, pl.ds(hidden, hidden)], q_ref))
    later.append((before_ref, earlier_ref))
    later.append((w_out_ref, out_buf))
    later.append((projected_ref.at[:, pl.ds(0, hidden)], gate_ref))
    later.append((events_hbm, events_ref))
    later = [
        pltpu.make_async_copy(source, target, sems.at[picks + num])
        for num, (source, target) in enumerate(later)
    ]
    acc_ref[...] = jnp.zeros_like(acc_ref)
    for copy in copies:
        copy.wait()
    later[0].start()
    later[1].start()
    normed = centered(rows_ref[...].astype(F32)).astype(BF16)
    for part in range(parts):
        later[part].wait()
        if part + 2 < parts:
            later[part + 2].start()
        else:
            for copy in later[parts + 3 * (part + 2 - parts) :][:3]:
                copy.start()
        for piece in range(2):
            columns = pl.ds(part * step + piece * (step // 2), step // 2)
            value = jnp.dot(normed, w_buf[:, columns], preferred_element_type=F32)
            pair_ref[:, columns] = silu_of_half(0.5 * value).astype(BF16)
    later[parts].wait()

    base = time_base(me, count, rows)
    first_start = starts_of(base, lengths_ref)
    gap = iota((LANES, LANES), 0) - iota((LANES, LANES), 1)
    width = 4 * head_size
    scaled = head_rows(head_size, width, 0.5 * head_size**-0.5)
    chosen = head_rows(head_size, width, 1.0)
    tiles = rows // LANES

    @pl.loop(0, picks)
    def _(pick):
        away = lists_ref[0, pick]
        block = lax.rem(me - away + count, count)
        key_base = time_base(block, count, rows)
        useful = (key_base < base) & (key_base + rows - 1 >= first_start)

        @pl.when(useful)
        def _():
            start = starts_of(base + iota((rows, LANES), 0), lengths_ref)
            for tile in range(tiles):
                key_time = key_base + tile * LANES + iota((rows, LANES), 1)
                mask_ref[:, tile * LANES : (tile + 1) * LANES] = jnp.where(
                    key_time >= start, 0.0, BLOCKED
                )
            lows, highs = {}, {}
            for diff in range(1 - tiles, tiles):
                delta = away * rows + diff * LANES
                bucket, power = jnp.int32(8), jnp.int32(0)
                for degree in range(8, rel_ref.shape[1] - 1):
                    bucket = bucket + (delta >= 2**degree).astype(jnp.int32)
                    power = power + (delta == 2**degree).astype(jnp.int32)
                highs[diff] = bucket
                lows[diff] = bucket - power
            special = 1 - tiles

            @pl.when(away == 1)
            def _():
                @pl.loop(0, head_count)
                def _(head):
                    near_ref[head] = bias_chain(gap + LANES, rel_ref, head, 1, 1, 8)

            @pl.when(away != 1)
            def _():
                @pl.loop(0, head_count)
                def _(head):
                    near_ref[head] = jnp.full(
                        gap.shape, half_bias(rel_ref, head, highs[special]), F32
                    )

            key_rows = pl.ds(pl.multiple_of(pick * rows, rows), rows)
            for group in range(hidden // width):
                columns = slice(group * width, (group + 1) * width)
                queries = q_ref[:, columns]
                values = pair_ref[key_rows, columns]
                keys = pair_ref[key_rows, hidden + group * width : hidden + (group + 1) * width]
                weights, stacked = [], []
                for num in range(width // head_size):
                    head = group * (width // head_size) + num
                    scores = lax.dot_general(
                        queries * scaled[num], keys, NT, preferred_element_type=F32
                    )
                    lines = []
                    for q_tile in range(tiles):
                        line = []
                        for k_tile in range(tiles):
                            diff = q_tile - k_tile
                            if diff == special:
                                bias = near_ref[head]
                            elif diff in (0, 2 - tiles):
                                bias = jnp.where(
                                    gap >= 0,
                                    half_bias(rel_ref, head, highs[diff]),
                                    half_bias(rel_ref, head, lows[diff]),
                                )
                            else:
                                bias = half_bias(rel_ref, head, highs[diff])
                            spot = (
                                slice(q_tile * LANES, (q_tile + 1) * LANES),
                                slice(k_tile * LANES, (k_tile + 1) * LANES),
                            )
                            line.append(
                                silu_of_half(scores[spot] + bias + mask_ref[spot]).astype(BF16)
                            )
                        lines.append(jnp.concatenate(line, 1))
                    weights.append(jnp.concatenate(lines, 0))
                    stacked.append(values * chosen[num])
                acc_ref[:, columns] += jnp.dot(
                    jnp.concatenate(weights, 1),
                    jnp.concatenate(stacked, 0),
                    preferred_element_type=F32,
                )

    later[parts + 1].wait()
    diagonal = iota((LANES, LANES), 0) == iota((LANES, LANES), 1)
    for copy in later[parts + 2 :]:
        copy.wait()
    scale = hidden**-0.5
    total = count * rows
    departures = []
    for part in range(2):
        block_rows = slice(part * half, (part + 1) * half)
        attended = acc_ref[block_rows] + earlier_ref[block_rows]
        gated = centered(attended) * gate_ref[block_rows].astype(F32)
        layer = events_ref[block_rows].astype(F32) + jnp.dot(
            gated.astype(BF16), out_buf[...], preferred_element_type=F32
        )
        layer = layer.astype(BF16)
        layer_ref[block_rows] = layer
        leaving = pltpu.make_async_copy(
            layer_ref.at[pl.ds(part * half, half)],
            layer_hbm.at[pl.ds(part * half, half)],
            layer_sems.at[part],
        )
        leaving.start()
        departures.append(leaving)
        following = pltpu.roll(events_ref[block_rows].astype(F32), half - 1, 0)
        if part == 0:
            after = events_ref[half : half + 16][:1].astype(F32)
        else:
            after = next_ref[...].astype(F32)
        following = jnp.where(iota((half, hidden), 0) == half - 1, after, following)
        inner = jnp.sum(layer.astype(F32) * following, 1, keepdims=True) * scale
        for tile in range(half // LANES):
            spot = inner[tile * LANES : (tile + 1) * LANES]
            line = jnp.sum(jnp.where(diagonal, spot, 0.0), 0, keepdims=True)
            offset = part * half + tile * LANES
            coming = base + offset + 1 + iota((1, LANES), 1)
            same = coming < total
            end = jnp.int32(0)
            for user in range(lengths_ref.shape[0]):
                end = end + lengths_ref[user]
                same = same & (coming != end)
            score_ref[offset // LANES : offset // LANES + 1] = jnp.where(same, line, 0.0)
    for leaving in departures:
        leaving.wait()


def table_kernel(slot_cap, layer_hbm, flat_ref, cand_ref, table_ref, layer_ref, sem):
    arrival = pltpu.make_async_copy(layer_hbm, layer_ref, sem)
    arrival.start()
    me = lax.axis_index("ctx")
    rows, hidden = layer_ref.shape
    wanted = cand_ref.shape[1]
    own = jnp.broadcast_to(cand_ref[pl.ds(me, 1), :].astype(F32), (wanted, wanted))
    diagonal = iota((wanted, wanted), 0) == iota((wanted, wanted), 1)
    own_column = jnp.sum(jnp.where(diagonal, own, 0.0), 1, keepdims=True)
    owner = jnp.floor(own * (1.0 / rows))
    owner_column = jnp.floor(own_column * (1.0 / rows))
    before = iota((wanted, wanted), 1) < iota((wanted, wanted), 0)
    rank = jnp.sum(jnp.where((owner == owner_column) & before, 1.0, 0.0), 1, keepdims=True)
    slot = (owner_column * slot_cap + rank).astype(jnp.int32)
    hits = (slot == iota((wanted, flat_ref.shape[0]), 1)).astype(BF16)
    listed = jnp.dot(hits, flat_ref[...], preferred_element_type=F32).astype(BF16)
    arrival.wait()
    scores = lax.dot_general(layer_ref[...], listed, NT, preferred_element_type=F32)
    table_ref[...] = scores * hidden**-0.5


def smem():
    return pl.BlockSpec(memory_space=pltpu.SMEM)


def vmem():
    return pl.BlockSpec(memory_space=pltpu.VMEM)


def hbm():
    return pl.BlockSpec(memory_space=pltpu.HBM)


def anywhere():
    return pl.BlockSpec(memory_space=pl.ANY)


def placed(value):
    return pltpu.with_memory_space_constraint(value, pltpu.HBM)


def params(mebibytes, *semantics):
    return pltpu.CompilerParams(
        dimension_semantics=semantics or None, vmem_limit_bytes=mebibytes * 2**20
    )


def shards(events, w_in, w_out, rel_bias, lengths, block_lists, candidates):
    rows, hidden = events.shape
    head_count = rel_bias.shape[0]
    head_size = hidden // head_count
    count = lax.axis_size("ctx")
    wanted = candidates.shape[1]
    slot_cap = 2 * wanted // count
    slots = count * slot_cap
    half = rows // 2
    width = 4 * head_size
    picks = block_lists.shape[1]

    ring = range(count)
    across_pairs = [(s, s ^ 2) for s in ring]
    over_pairs = [(s, (s + 2) % count) for s in ring]
    far_pairs = [(s, (s + 4) % count) for s in ring]
    passing_pairs = [(s, (s + 4) % count) for s in ring if s % 4 < 2]
    back_pairs = [(s, (s - 1) % count) for s in ring]
    up_pairs = [(s, s + 1) for s in ring if s % 2 == 0]
    down_pairs = [(s, s - 1) for s in ring if s % 2 == 1]
    twin_pairs = [(s, s ^ 1) for s in ring]
    upper_twins = [(s, s ^ 1) for s in ring if s % 4 >= 2]
    lower_twins = [(s, s ^ 1) for s in ring if s % 4 < 2]

    next_first = passed_along(events[:1], back_pairs)
    own_twin = passed_along(events, up_pairs)
    across = passed_along(events[:half], across_pairs)
    far = passed_along(events, far_pairs)

    fetched, kept, attended, bottom = pl.pallas_call(
        functools.partial(front_kernel, head_size, slot_cap),
        out_shape=(
            jax.ShapeDtypeStruct((slots, hidden), BF16),
            pltpu.HBM((rows, 2 * hidden), BF16),
            pltpu.HBM((rows, hidden), F32),
            pltpu.HBM((half, hidden), BF16),
        ),
        in_specs=[smem(), smem(), vmem(), hbm(), hbm()],
        out_specs=(vmem(), hbm(), hbm(), hbm()),
        scratch_shapes=[
            pltpu.VMEM((rows, hidden), BF16),
            pltpu.VMEM((hidden, 4 * hidden), BF16),
            pltpu.VMEM((rows, 4 * hidden), BF16),
            pltpu.VMEM((rows, hidden), F32),
            pltpu.VMEM((rows, rows), F32),
            pltpu.SemaphoreType.DMA((9,)),
            pltpu.SemaphoreType.DMA((3,)),
        ],
        compiler_params=params(48),
        cost_estimate=pl.CostEstimate(
            flops=14 * 10**9, bytes_accessed=2**23, transcendentals=0
        ),
        name="front",
    )(placed(lengths), placed(rel_bias), placed(candidates), placed(events), placed(w_in))

    across, kept = lax.optimization_barrier((across, kept))
    far, attended = lax.optimization_barrier((far, attended))
    passed = passed_along(across, passing_pairs)
    over = passed_along(bottom, over_pairs)
    over_done, passed_done, fetched = lax.optimization_barrier((over, passed, fetched))
    across_twin = passed_along(across, upper_twins)
    over_twin = passed_along(over_done, twin_pairs)
    far_twin = passed_along(far, down_pairs)
    passed_twin = passed_along(passed_done, lower_twins)
    arrived = lax.all_to_all(
        fetched.reshape(count, slot_cap, hidden), "ctx", split_axis=0, concat_axis=0, tiled=True
    ).reshape(slots, hidden)

    parts = 4
    operands = [placed(kept), placed(attended), far, far_twin, own_twin, across]
    operands += [across_twin, passed_done, passed_twin, over_done, over_twin, placed(w_in), placed(events)]
    layer_output, next_score = pl.pallas_call(
        functools.partial(picks_kernel, head_size),
        out_shape=(
            pltpu.HBM((rows, hidden), BF16),
            jax.ShapeDtypeStruct((rows // LANES, LANES), F32),
        ),
        in_specs=[smem()] * 3 + [hbm()] * 2 + [anywhere()] * 9 + [hbm()] * 2 + [vmem(), hbm()],
        out_specs=(hbm(), vmem()),
        scratch_shapes=[
            pltpu.VMEM((rows, hidden), F32),
            pltpu.VMEM((rows, hidden), BF16),
            pltpu.VMEM((rows, hidden), F32),
            pltpu.VMEM((picks * rows, hidden), BF16),
            pltpu.VMEM((hidden, 2 * hidden), BF16),
            pltpu.VMEM((picks * rows, 2 * hidden), BF16),
            pltpu.VMEM((rows, rows), F32),
            pltpu.VMEM((head_count, LANES, LANES), F32),
            pltpu.SemaphoreType.DMA((picks + parts + 5,)),
            pltpu.VMEM((hidden, hidden), BF16),
            pltpu.VMEM((rows, hidden), BF16),
            pltpu.VMEM((rows, hidden), BF16),
            pltpu.VMEM((rows, hidden), BF16),
            pltpu.SemaphoreType.DMA((2,)),
        ],
        compiler_params=params(50),
        cost_estimate=pl.CostEstimate(
            flops=20 * 10**9, bytes_accessed=2**23, transcendentals=0
        ),
        name="picks",
    )(lengths, block_lists, rel_bias, *operands, next_first, placed(w_out))
    table = pl.pallas_call(
        functools.partial(table_kernel, slot_cap),
        out_shape=jax.ShapeDtypeStruct((rows, wanted), F32),
        in_specs=[hbm(), vmem(), vmem()],
        out_specs=vmem(),
        scratch_shapes=[pltpu.VMEM((rows, hidden), BF16), pltpu.SemaphoreType.DMA],
        compiler_params=params(10),
        cost_estimate=pl.CostEstimate(flops=10**9, bytes_accessed=2**21, transcendentals=0),
        name="table",
    )(placed(layer_output), arrived, candidates)
    return (layer_output, next_score.reshape(rows), table)


def solution(mesh):
    in_specs = (
        P(("groups", "ctx"), None),
        P(),
        P(),
        P(),
        P("groups"),
        P(("groups", "ctx"), None),
        P("groups", None),
    )
    out_specs = (P(("groups", "ctx"), None), P(("groups", "ctx")), P(("groups", "ctx"), None))
    return jax.shard_map(shards, mesh=mesh, in_specs=in_specs, out_specs=out_specs, check_vma=False)
```

```python
import functools

import jax
import jax.numpy as jnp
from jax import lax
from jax.experimental import pallas as pl
from jax.experimental.pallas import tpu as pltpu
from jax.sharding import PartitionSpec as P

BLOCKED = -1e9
LANES = 128
F32 = jnp.float32
BF16 = jnp.bfloat16
NT = (((1,), (1,)), ((), ()))


def passed_along(value, pairs):
    return lax.ppermute(value, "ctx", pairs)


def centered(values):
    center = values - jnp.mean(values, -1, keepdims=True)
    spread = jnp.mean(center * center, -1, keepdims=True)
    return center * lax.rsqrt(spread + 1e-05)


def silu_of_half(half):
    return half * jnp.tanh(half) + half


def iota(shape, dim):
    return lax.broadcasted_iota(jnp.int32, shape, dim)


def time_base(block, count, rows):
    total = count * rows
    return lax.rem(block * rows + total // 4, total)


def starts_of(times, lengths_ref):
    end = jnp.int32(0)
    start = jnp.zeros_like(times)
    for user in range(lengths_ref.shape[0]):
        length = lengths_ref[user]
        end = end + length
        start = start + jnp.where(times >= end, length, 0)
    return start


def half_bias(rel_ref, head, bucket):
    return rel_ref[head, bucket] * 0.5


def bias_chain(distance, rel_ref, head, low, first, last):
    tile = jnp.full(distance.shape, half_bias(rel_ref, head, low), F32)
    for degree in range(first, last):
        tile = jnp.where(distance >= 2**degree, half_bias(rel_ref, head, degree + 1), tile)
    return tile


def head_rows(size, width, value):
    lane = iota((1, width), 1)
    return [
        jnp.where((lane >= size * num) & (lane < size * (num + 1)), value, 0.0).astype(BF16)
        for num in range(width // size)
    ]


def requested_rows(slot_cap, cand_ref, events):
    me = lax.axis_index("ctx")
    count, wanted = cand_ref.shape
    rows = events.shape[0]
    slots = count * slot_cap
    cand = cand_ref[...]
    local = cand - me * rows
    mine = (local >= 0) & (local < rows)
    earlier = (iota((wanted, wanted), 0) < iota((wanted, wanted), 1)).astype(BF16)
    rank = jnp.dot(jnp.where(mine, 1.0, 0.0).astype(BF16), earlier, preferred_element_type=F32)
    code = jnp.where(mine, rank * rows + local.astype(F32), -1.0)
    slot_num = iota((slots, count), 0) - iota((slots, count), 1) * slot_cap
    spread = jnp.where((slot_num >= 0) & (slot_num < slot_cap), 1.0, 0.0)
    asked = jnp.dot(spread, code, preferred_element_type=F32, precision=lax.Precision.HIGHEST)
    slot = lax.rem(iota((slots, wanted), 0), slot_cap).astype(F32)
    found = asked - slot * rows
    ids = jnp.sum(jnp.where((found >= 0.0) & (found < rows), found + 1.0, 0.0), 1, keepdims=True)
    picks = (ids.astype(jnp.int32) - 1 == iota((slots, rows), 1)).astype(BF16)
    return jnp.dot(picks, events, preferred_element_type=F32).astype(BF16)


def slot_hits(slot_cap, rows, cand_ref):
    me = lax.axis_index("ctx")
    count = cand_ref.shape[0]
    wanted = cand_ref.shape[1]
    own = jnp.broadcast_to(cand_ref[pl.ds(me, 1), :].astype(F32), (wanted, wanted))
    diagonal = iota((wanted, wanted), 0) == iota((wanted, wanted), 1)
    own_column = jnp.sum(jnp.where(diagonal, own, 0.0), 1, keepdims=True)
    owner = jnp.floor(own * (1.0 / rows))
    owner_column = jnp.floor(own_column * (1.0 / rows))
    before = iota((wanted, wanted), 1) < iota((wanted, wanted), 0)
    rank = jnp.sum(jnp.where((owner == owner_column) & before, 1.0, 0.0), 1, keepdims=True)
    slot = (owner_column * slot_cap + rank).astype(jnp.int32)
    hits = (slot == iota((wanted, count * slot_cap), 1)).astype(BF16)
    return hits


def own_attention(head_size, lengths_ref, rel_ref, pair_buf, mask_ref, out_ref, finish):
    rows, hidden = out_ref.shape
    half = rows // 2
    width = 4 * head_size
    heads = width // head_size
    base = time_base(lax.axis_index("ctx"), lax.axis_size("ctx"), rows)
    start = starts_of(base + iota((rows, LANES), 0), lengths_ref)
    for num in range(rows // LANES):
        key_time = base + num * LANES + iota((rows, LANES), 1)
        mask_ref[:, num * LANES : (num + 1) * LANES] = jnp.where(key_time >= start, 0.0, BLOCKED)
    away = iota((LANES, LANES), 0) - iota((LANES, LANES), 1)
    scaled = head_rows(head_size, width, 0.5 * head_size**-0.5)
    chosen = head_rows(head_size, width, 1.0)
    for group in range(hidden // width):
        spot = slice(group * width, (group + 1) * width)
        queries, values, keys = [
            pair_buf[:, which * hidden + spot.start : which * hidden + spot.stop]
            for which in (1, 2, 3)
        ]
        parts = [([], []), ([], [])]
        for num in range(heads):
            head = group * heads + num
            tiles = [
                jnp.where(away < 0, BLOCKED, bias_chain(away, rel_ref, head, 0, 0, 7)),
                bias_chain(away + LANES, rel_ref, head, 1, 1, 8),
                jnp.where(away >= 0, half_bias(rel_ref, head, 9), half_bias(rel_ref, head, 8)),
                half_bias(rel_ref, head, 9),
            ]
            head_queries = queries * scaled[num]
            head_values = values * chosen[num]
            for part in range(2):
                seen = (part + 1) * half
                scores = lax.dot_general(
                    head_queries[part * half : (part + 1) * half],
                    keys[:seen],
                    NT,
                    preferred_element_type=F32,
                )
                lines = []
                for q_sub in range(half // LANES):
                    q_tile = part * (half // LANES) + q_sub
                    line = []
                    for k_tile in range(seen // LANES):
                        if k_tile > q_tile:
                            line.append(jnp.zeros((LANES, LANES), BF16))
                            continue
                        k_spot = slice(k_tile * LANES, (k_tile + 1) * LANES)
                        part_scores = scores[q_sub * LANES : (q_sub + 1) * LANES, k_spot]
                        mask = mask_ref[q_tile * LANES : (q_tile + 1) * LANES, k_spot]
                        line.append(
                            silu_of_half(part_scores + tiles[q_tile - k_tile] + mask).astype(BF16)
                        )
                    lines.append(jnp.concatenate(line, 1))
                parts[part][0].append(jnp.concatenate(lines, 0))
                parts[part][1].append(head_values[:seen])
        for part in range(2):
            out_ref[part * half : (part + 1) * half, spot] = jnp.dot(
                jnp.concatenate(parts[part][0], 1),
                jnp.concatenate(parts[part][1], 0),
                preferred_element_type=F32,
            )
    finish()


def front_kernel(head_size, slot_cap, *refs):
    lengths_ref, rel_ref, cand_ref, events_hbm, w_ref = refs[:5]
    sent_ref, hits_ref, kept_hbm, attended_hbm, bottom_hbm = refs[5:10]
    events_ref, w_buf, pair_buf, out_buf, mask_ref, in_sems, out_sems = refs[10:]
    rows, hidden = events_ref.shape
    half = rows // 2
    step = hidden // 2
    arrival = pltpu.make_async_copy(events_hbm, events_ref, in_sems.at[8])
    arrival.start()
    order = [2, 3, 6, 7, 4, 5, 0, 1]
    arrivals = [
        pltpu.make_async_copy(
            w_ref.at[:, pl.ds(part * step, step)],
            w_buf.at[:, pl.ds(part * step, step)],
            in_sems.at[part],
        )
        for part in order
    ]
    bottom = pltpu.make_async_copy(events_ref.at[pl.ds(half, half)], bottom_hbm, out_sems.at[0])
    kept = pltpu.make_async_copy(pair_buf.at[:, pl.ds(0, 2 * hidden)], kept_hbm, out_sems.at[1])
    attended = pltpu.make_async_copy(out_buf, attended_hbm, out_sems.at[2])
    ahead = 2
    for copy in arrivals[:ahead]:
        copy.start()
    arrival.wait()
    bottom.start()
    normed = centered(events_ref[...].astype(F32)).astype(BF16)
    for num, part in enumerate(order):
        arrivals[num].wait()
        if num + ahead < len(arrivals):
            arrivals[num + ahead].start()
        spot = slice(part * step, (part + 1) * step)
        value = jnp.dot(normed, w_buf[:, spot], preferred_element_type=F32)
        pair_buf[:, spot] = silu_of_half(0.5 * value).astype(BF16)
    kept.start()
    sent_ref[...] = requested_rows(slot_cap, cand_ref, events_ref[...])
    hits_ref[...] = slot_hits(slot_cap, rows, cand_ref)
    own_attention(head_size, lengths_ref, rel_ref, pair_buf, mask_ref, out_buf, attended.start)
    for copy in (bottom, kept, attended):
        copy.wait()


def picks_kernel(head_size, *refs):
    lengths_ref, lists_ref, rel_ref, projected_ref, before_ref = refs[:5]
    far_ref, far_twin_ref, own_twin_ref, across_ref, across_twin_ref = refs[5:10]
    passed_ref, passed_twin_ref, over_ref, over_twin_ref, w_ref = refs[10:15]
    events_hbm, next_ref, w_out_ref = refs[15:18]
    layer_hbm, score_ref = refs[18:20]
    acc_ref, q_ref, rows_ref, w_buf, pair_ref, mask_ref, near_ref = refs[20:27]
    sems, out_buf, gate_ref, events_ref, layer_ref, layer_sems = refs[27:]
    me = lax.axis_index("ctx")
    count = lax.axis_size("ctx")
    rows, hidden = q_ref.shape
    half = rows // 2
    picks = lists_ref.shape[1]
    head_count, _ = rel_ref.shape
    second = lax.rem(me, 2) == 1
    first = jnp.logical_not(second)
    upper = lax.rem(me, 4) >= 2
    lower = jnp.logical_not(upper)

    copies = []
    for pick in range(picks):
        away = lists_ref[0, pick]
        crossed = ((away == 1) & first) | ((away == 3) & second)
        target = rows_ref.at[pl.ds(pick * rows, rows)]
        head = rows_ref.at[pl.ds(pick * rows, half)]
        tail = rows_ref.at[pl.ds(pick * rows + half, half)]
        sources = [
            (away == 4, far_ref, target),
            ((away == 3) & first, far_twin_ref, target),
            ((away == 1) & second, own_twin_ref, target),
            ((away == 2) & upper, across_ref, head),
            ((away == 2) & lower, passed_ref, head),
            (away == 2, over_ref, tail),
            (crossed & upper, across_twin_ref, head),
            (crossed & lower, passed_twin_ref, head),
            (crossed, over_twin_ref, tail),
        ]
        for flag, source, spot in sources:

            @pl.when(flag)
            def _():
                pltpu.make_async_copy(source, spot, sems.at[pick]).start()

        copies.append(pltpu.make_async_copy(far_ref, target, sems.at[pick]))
    step = hidden // 2
    parts = 2 * hidden // step
    later = [
        (w_ref.at[:, pl.ds(2 * hidden + part * step, step)], w_buf.at[:, pl.ds(part * step, step)])
        for part in range(parts)
    ]
    later.append((projected_ref.at[:, pl.ds(hidden, hidden)], q_ref))
    later.append((before_ref, acc_ref))
    later.append((w_out_ref, out_buf))
    later.append((projected_ref.at[:, pl.ds(0, hidden)], gate_ref))
    later.append((events_hbm, events_ref))
    later = [
        pltpu.make_async_copy(source, target, sems.at[picks + num])
        for num, (source, target) in enumerate(later)
    ]
    for copy in copies:
        copy.wait()
    later[0].start()
    later[1].start()
    normed = centered(rows_ref[...].astype(F32)).astype(BF16)
    for part in range(parts):
        later[part].wait()
        if part + 2 < parts:
            later[part + 2].start()
        else:
            for copy in later[parts + 3 * (part + 2 - parts) :][:3]:
                copy.start()
        columns = pl.ds(part * step, step)
        value = jnp.dot(normed, w_buf[:, columns], preferred_element_type=F32)
        pair_ref[:, columns] = silu_of_half(0.5 * value).astype(BF16)
    later[parts].wait()
    later[parts + 1].wait()

    base = time_base(me, count, rows)
    first_start = starts_of(base, lengths_ref)
    gap = iota((LANES, LANES), 0) - iota((LANES, LANES), 1)
    width = 4 * head_size
    scaled = head_rows(head_size, width, 0.5 * head_size**-0.5)
    chosen = head_rows(head_size, width, 1.0)
    tiles = rows // LANES

    @pl.loop(0, picks)
    def _(pick):
        away = lists_ref[0, pick]
        block = lax.rem(me - away + count, count)
        key_base = time_base(block, count, rows)
        useful = (key_base < base) & (key_base + rows - 1 >= first_start)

        @pl.when(useful)
        def _():
            start = starts_of(base + iota((rows, LANES), 0), lengths_ref)
            for tile in range(tiles):
                key_time = key_base + tile * LANES + iota((rows, LANES), 1)
                mask_ref[:, tile * LANES : (tile + 1) * LANES] = jnp.where(
                    key_time >= start, 0.0, BLOCKED
                )
            lows, highs = {}, {}
            for diff in range(1 - tiles, tiles):
                delta = away * rows + diff * LANES
                bucket, power = jnp.int32(8), jnp.int32(0)
                for degree in range(8, rel_ref.shape[1] - 1):
                    bucket = bucket + (delta >= 2**degree).astype(jnp.int32)
                    power = power + (delta == 2**degree).astype(jnp.int32)
                highs[diff] = bucket
                lows[diff] = bucket - power
            special = 1 - tiles

            @pl.when(away == 1)
            def _():
                @pl.loop(0, head_count)
                def _(head):
                    near_ref[head] = bias_chain(gap + LANES, rel_ref, head, 1, 1, 8)

            @pl.when(away != 1)
            def _():
                @pl.loop(0, head_count)
                def _(head):
                    near_ref[head] = jnp.full(
                        gap.shape, half_bias(rel_ref, head, highs[special]), F32
                    )

            key_rows = pl.ds(pl.multiple_of(pick * rows, rows), rows)
            for group in range(hidden // width):
                columns = slice(group * width, (group + 1) * width)
                queries = q_ref[:, columns]
                values = pair_ref[key_rows, columns]
                keys = pair_ref[key_rows, hidden + group * width : hidden + (group + 1) * width]
                weights, stacked = [], []
                for num in range(width // head_size):
                    head = group * (width // head_size) + num
                    scores = lax.dot_general(
                        queries * scaled[num], keys, NT, preferred_element_type=F32
                    )
                    lines = []
                    for q_tile in range(tiles):
                        line = []
                        for k_tile in range(tiles):
                            diff = q_tile - k_tile
                            if diff == special:
                                bias = near_ref[head]
                            elif diff in (0, 2 - tiles):
                                bias = jnp.where(
                                    gap >= 0,
                                    half_bias(rel_ref, head, highs[diff]),
                                    half_bias(rel_ref, head, lows[diff]),
                                )
                            else:
                                bias = half_bias(rel_ref, head, highs[diff])
                            spot = (
                                slice(q_tile * LANES, (q_tile + 1) * LANES),
                                slice(k_tile * LANES, (k_tile + 1) * LANES),
                            )
                            line.append(
                                silu_of_half(scores[spot] + bias + mask_ref[spot]).astype(BF16)
                            )
                        lines.append(jnp.concatenate(line, 1))
                    weights.append(jnp.concatenate(lines, 0))
                    stacked.append(values * chosen[num])
                acc_ref[:, columns] += jnp.dot(
                    jnp.concatenate(weights, 1),
                    jnp.concatenate(stacked, 0),
                    preferred_element_type=F32,
                )

    diagonal = iota((LANES, LANES), 0) == iota((LANES, LANES), 1)
    for copy in later[parts + 2 :]:
        copy.wait()
    scale = hidden**-0.5
    total = count * rows
    departures = []
    for part in range(2):
        block_rows = slice(part * half, (part + 1) * half)
        gated = centered(acc_ref[block_rows]) * gate_ref[block_rows].astype(F32)
        layer = events_ref[block_rows].astype(F32) + jnp.dot(
            gated.astype(BF16), out_buf[...], preferred_element_type=F32
        )
        layer = layer.astype(BF16)
        layer_ref[block_rows] = layer
        leaving = pltpu.make_async_copy(
            layer_ref.at[pl.ds(part * half, half)],
            layer_hbm.at[pl.ds(part * half, half)],
            layer_sems.at[part],
        )
        leaving.start()
        departures.append(leaving)
        following = pltpu.roll(events_ref[block_rows].astype(F32), half - 1, 0)
        if part == 0:
            after = events_ref[half : half + 16][:1].astype(F32)
        else:
            after = next_ref[...].astype(F32)
        following = jnp.where(iota((half, hidden), 0) == half - 1, after, following)
        inner = jnp.sum(layer.astype(F32) * following, 1, keepdims=True) * scale
        for tile in range(half // LANES):
            spot = inner[tile * LANES : (tile + 1) * LANES]
            line = jnp.sum(jnp.where(diagonal, spot, 0.0), 0, keepdims=True)
            offset = part * half + tile * LANES
            coming = base + offset + 1 + iota((1, LANES), 1)
            same = coming < total
            end = jnp.int32(0)
            for user in range(lengths_ref.shape[0]):
                end = end + lengths_ref[user]
                same = same & (coming != end)
            score_ref[offset // LANES : offset // LANES + 1] = jnp.where(same, line, 0.0)
    for leaving in departures:
        leaving.wait()


def table_kernel(layer_hbm, flat_hbm, hits_ref, table_ref, layer_ref, flat_ref, sems):
    flat_arrival = pltpu.make_async_copy(flat_hbm, flat_ref, sems.at[0])
    flat_arrival.start()
    arrival = pltpu.make_async_copy(layer_hbm, layer_ref, sems.at[1])
    arrival.start()
    flat_arrival.wait()
    listed = jnp.dot(hits_ref[...], flat_ref[...], preferred_element_type=F32).astype(BF16)
    arrival.wait()
    scores = lax.dot_general(layer_ref[...], listed, NT, preferred_element_type=F32)
    table_ref[...] = scores * layer_ref.shape[1] ** -0.5


def smem():
    return pl.BlockSpec(memory_space=pltpu.SMEM)


def vmem():
    return pl.BlockSpec(memory_space=pltpu.VMEM)


def hbm():
    return pl.BlockSpec(memory_space=pltpu.HBM)


def anywhere():
    return pl.BlockSpec(memory_space=pl.ANY)


def placed(value):
    return pltpu.with_memory_space_constraint(value, pltpu.HBM)


def params(mebibytes, *semantics):
    return pltpu.CompilerParams(
        dimension_semantics=semantics or None, vmem_limit_bytes=mebibytes * 2**20
    )


def shards(events, w_in, w_out, rel_bias, lengths, block_lists, candidates):
    rows, hidden = events.shape
    head_count = rel_bias.shape[0]
    head_size = hidden // head_count
    count = lax.axis_size("ctx")
    wanted = candidates.shape[1]
    slot_cap = 2 * wanted // count
    slots = count * slot_cap
    half = rows // 2
    width = 4 * head_size
    picks = block_lists.shape[1]

    ring = range(count)
    across_pairs = [(s, s ^ 2) for s in ring]
    over_pairs = [(s, (s + 2) % count) for s in ring]
    far_pairs = [(s, (s + 4) % count) for s in ring]
    passing_pairs = [(s, (s + 4) % count) for s in ring if s % 4 < 2]
    back_pairs = [(s, (s - 1) % count) for s in ring]
    up_pairs = [(s, s + 1) for s in ring if s % 2 == 0]
    down_pairs = [(s, s - 1) for s in ring if s % 2 == 1]
    twin_pairs = [(s, s ^ 1) for s in ring]
    upper_twins = [(s, s ^ 1) for s in ring if s % 4 >= 2]
    lower_twins = [(s, s ^ 1) for s in ring if s % 4 < 2]

    next_first = passed_along(events[:1], back_pairs)
    own_twin = passed_along(events, up_pairs)
    across = passed_along(events[:half], across_pairs)
    far = passed_along(events, far_pairs)

    fetched, hits, kept, attended, bottom = pl.pallas_call(
        functools.partial(front_kernel, head_size, slot_cap),
        out_shape=(
            jax.ShapeDtypeStruct((slots, hidden), BF16),
            jax.ShapeDtypeStruct((wanted, slots), BF16),
            pltpu.HBM((rows, 2 * hidden), BF16),
            pltpu.HBM((rows, hidden), F32),
            pltpu.HBM((half, hidden), BF16),
        ),
        in_specs=[smem(), smem(), vmem(), hbm(), hbm()],
        out_specs=(vmem(), vmem(), hbm(), hbm(), hbm()),
        scratch_shapes=[
            pltpu.VMEM((rows, hidden), BF16),
            pltpu.VMEM((hidden, 4 * hidden), BF16),
            pltpu.VMEM((rows, 4 * hidden), BF16),
            pltpu.VMEM((rows, hidden), F32),
            pltpu.VMEM((rows, rows), F32),
            pltpu.SemaphoreType.DMA((9,)),
            pltpu.SemaphoreType.DMA((3,)),
        ],
        compiler_params=params(48),
        cost_estimate=pl.CostEstimate(
            flops=14 * 10**9, bytes_accessed=2**23, transcendentals=0
        ),
        name="front",
    )(placed(lengths), placed(rel_bias), placed(candidates), placed(events), placed(w_in))

    across, kept = lax.optimization_barrier((across, kept))
    far, attended = lax.optimization_barrier((far, attended))
    passed = passed_along(across, passing_pairs)
    over = passed_along(bottom, over_pairs)
    over_done, passed_done, fetched = lax.optimization_barrier((over, passed, fetched))
    across_twin = passed_along(across, upper_twins)
    over_twin = passed_along(over_done, twin_pairs)
    far_twin = passed_along(far, down_pairs)
    passed_twin = passed_along(passed_done, lower_twins)
    arrived = lax.all_to_all(
        fetched.reshape(count, slot_cap, hidden), "ctx", split_axis=0, concat_axis=0, tiled=True
    ).reshape(slots, hidden)

    parts = 4
    operands = [placed(kept), placed(attended), far, far_twin, own_twin, across]
    operands += [across_twin, passed_done, passed_twin, over_done, over_twin, placed(w_in), placed(events)]
    layer_output, next_score = pl.pallas_call(
        functools.partial(picks_kernel, head_size),
        out_shape=(
            pltpu.HBM((rows, hidden), BF16),
            jax.ShapeDtypeStruct((rows // LANES, LANES), F32),
        ),
        in_specs=[smem()] * 3 + [hbm()] * 2 + [anywhere()] * 9 + [hbm()] * 2 + [vmem(), hbm()],
        out_specs=(hbm(), vmem()),
        scratch_shapes=[
            pltpu.VMEM((rows, hidden), F32),
            pltpu.VMEM((rows, hidden), BF16),
            pltpu.VMEM((picks * rows, hidden), BF16),
            pltpu.VMEM((hidden, 2 * hidden), BF16),
            pltpu.VMEM((picks * rows, 2 * hidden), BF16),
            pltpu.VMEM((rows, rows), F32),
            pltpu.VMEM((head_count, LANES, LANES), F32),
            pltpu.SemaphoreType.DMA((picks + parts + 5,)),
            pltpu.VMEM((hidden, hidden), BF16),
            pltpu.VMEM((rows, hidden), BF16),
            pltpu.VMEM((rows, hidden), BF16),
            pltpu.VMEM((rows, hidden), BF16),
            pltpu.SemaphoreType.DMA((2,)),
        ],
        compiler_params=params(50),
        cost_estimate=pl.CostEstimate(
            flops=20 * 10**9, bytes_accessed=2**23, transcendentals=0
        ),
        name="picks",
    )(lengths, block_lists, rel_bias, *operands, next_first, placed(w_out))
    table = pl.pallas_call(
        table_kernel,
        out_shape=jax.ShapeDtypeStruct((rows, wanted), F32),
        in_specs=[hbm(), anywhere(), vmem()],
        out_specs=vmem(),
        scratch_shapes=[
            pltpu.VMEM((rows, hidden), BF16),
            pltpu.VMEM((slots, hidden), BF16),
            pltpu.SemaphoreType.DMA((2,)),
        ],
        compiler_params=params(10),
        cost_estimate=pl.CostEstimate(flops=10**9, bytes_accessed=2**21, transcendentals=0),
        name="table",
    )(placed(layer_output), arrived, hits)
    return (layer_output, next_score.reshape(rows), table)


def solution(mesh):
    in_specs = (
        P(("groups", "ctx"), None),
        P(),
        P(),
        P(),
        P("groups"),
        P(("groups", "ctx"), None),
        P("groups", None),
    )
    out_specs = (P(("groups", "ctx"), None), P(("groups", "ctx")), P(("groups", "ctx"), None))
    return jax.shard_map(shards, mesh=mesh, in_specs=in_specs, out_specs=out_specs, check_vma=False)
```

```python
import functools

import jax
import jax.numpy as jnp
from jax import lax
from jax.experimental import pallas as pl
from jax.experimental.pallas import tpu as pltpu
from jax.sharding import PartitionSpec as P

BLOCKED = -1e9
LANES = 128
F32 = jnp.float32
BF16 = jnp.bfloat16
NT = (((1,), (1,)), ((), ()))


def passed_along(value, pairs):
    return lax.ppermute(value, "ctx", pairs)


def centered(values):
    center = values - jnp.mean(values, -1, keepdims=True)
    spread = jnp.mean(center * center, -1, keepdims=True)
    return center * lax.rsqrt(spread + 1e-05)


def silu_of_half(half):
    return half * jnp.tanh(half) + half


def iota(shape, dim):
    return lax.broadcasted_iota(jnp.int32, shape, dim)


def time_base(block, count, rows):
    total = count * rows
    return lax.rem(block * rows + total // 4, total)


def starts_of(times, lengths_ref):
    end = jnp.int32(0)
    start = jnp.zeros_like(times)
    for user in range(lengths_ref.shape[0]):
        length = lengths_ref[user]
        end = end + length
        start = start + jnp.where(times >= end, length, 0)
    return start


def half_bias(rel_ref, head, bucket):
    return rel_ref[head, bucket] * 0.5


def bias_chain(distance, rel_ref, head, low, first, last):
    tile = jnp.full(distance.shape, half_bias(rel_ref, head, low), F32)
    for degree in range(first, last):
        tile = jnp.where(distance >= 2**degree, half_bias(rel_ref, head, degree + 1), tile)
    return tile


def head_rows(size, width, value):
    lane = iota((1, width), 1)
    return [
        jnp.where((lane >= size * num) & (lane < size * (num + 1)), value, 0.0).astype(BF16)
        for num in range(width // size)
    ]


def requested_rows(slot_cap, cand_ref, events):
    me = lax.axis_index("ctx")
    count, wanted = cand_ref.shape
    rows = events.shape[0]
    slots = count * slot_cap
    cand = cand_ref[...]
    local = cand - me * rows
    mine = (local >= 0) & (local < rows)
    earlier = (iota((wanted, wanted), 0) < iota((wanted, wanted), 1)).astype(BF16)
    rank = jnp.dot(jnp.where(mine, 1.0, 0.0).astype(BF16), earlier, preferred_element_type=F32)
    code = jnp.where(mine, rank * rows + local.astype(F32), -1.0)
    slot_num = iota((slots, count), 0) - iota((slots, count), 1) * slot_cap
    spread = jnp.where((slot_num >= 0) & (slot_num < slot_cap), 1.0, 0.0)
    asked = jnp.dot(spread, code, preferred_element_type=F32, precision=lax.Precision.HIGHEST)
    slot = lax.rem(iota((slots, wanted), 0), slot_cap).astype(F32)
    found = asked - slot * rows
    ids = jnp.sum(jnp.where((found >= 0.0) & (found < rows), found + 1.0, 0.0), 1, keepdims=True)
    picks = (ids.astype(jnp.int32) - 1 == iota((slots, rows), 1)).astype(BF16)
    return jnp.dot(picks, events, preferred_element_type=F32).astype(BF16)


def slot_hits(slot_cap, rows, cand_ref):
    me = lax.axis_index("ctx")
    count = cand_ref.shape[0]
    wanted = cand_ref.shape[1]
    own = jnp.broadcast_to(cand_ref[pl.ds(me, 1), :].astype(F32), (wanted, wanted))
    diagonal = iota((wanted, wanted), 0) == iota((wanted, wanted), 1)
    own_column = jnp.sum(jnp.where(diagonal, own, 0.0), 1, keepdims=True)
    owner = jnp.floor(own * (1.0 / rows))
    owner_column = jnp.floor(own_column * (1.0 / rows))
    before = iota((wanted, wanted), 1) < iota((wanted, wanted), 0)
    rank = jnp.sum(jnp.where((owner == owner_column) & before, 1.0, 0.0), 1, keepdims=True)
    slot = (owner_column * slot_cap + rank).astype(jnp.int32)
    hits = (slot == iota((wanted, count * slot_cap), 1)).astype(BF16)
    return hits


def own_attention(head_size, lengths_ref, rel_ref, pair_buf, mask_ref, out_ref, finish):
    rows, hidden = out_ref.shape
    half = rows // 2
    width = 4 * head_size
    heads = width // head_size
    base = time_base(lax.axis_index("ctx"), lax.axis_size("ctx"), rows)
    start = starts_of(base + iota((rows, LANES), 0), lengths_ref)
    for num in range(rows // LANES):
        key_time = base + num * LANES + iota((rows, LANES), 1)
        mask_ref[:, num * LANES : (num + 1) * LANES] = jnp.where(key_time >= start, 0.0, BLOCKED)
    away = iota((LANES, LANES), 0) - iota((LANES, LANES), 1)
    scaled = head_rows(head_size, width, 0.5 * head_size**-0.5)
    chosen = head_rows(head_size, width, 1.0)
    for group in range(hidden // width):
        spot = slice(group * width, (group + 1) * width)
        queries, values, keys = [
            pair_buf[:, which * hidden + spot.start : which * hidden + spot.stop]
            for which in (1, 2, 3)
        ]
        parts = [([], []), ([], [])]
        for num in range(heads):
            head = group * heads + num
            tiles = [
                jnp.where(away < 0, BLOCKED, bias_chain(away, rel_ref, head, 0, 0, 7)),
                bias_chain(away + LANES, rel_ref, head, 1, 1, 8),
                jnp.where(away >= 0, half_bias(rel_ref, head, 9), half_bias(rel_ref, head, 8)),
                half_bias(rel_ref, head, 9),
            ]
            head_queries = queries * scaled[num]
            head_values = values * chosen[num]
            for part in range(2):
                seen = (part + 1) * half
                scores = lax.dot_general(
                    head_queries[part * half : (part + 1) * half],
                    keys[:seen],
                    NT,
                    preferred_element_type=F32,
                )
                lines = []
                for q_sub in range(half // LANES):
                    q_tile = part * (half // LANES) + q_sub
                    line = []
                    for k_tile in range(seen // LANES):
                        if k_tile > q_tile:
                            line.append(jnp.zeros((LANES, LANES), BF16))
                            continue
                        k_spot = slice(k_tile * LANES, (k_tile + 1) * LANES)
                        part_scores = scores[q_sub * LANES : (q_sub + 1) * LANES, k_spot]
                        mask = mask_ref[q_tile * LANES : (q_tile + 1) * LANES, k_spot]
                        line.append(
                            silu_of_half(part_scores + tiles[q_tile - k_tile] + mask).astype(BF16)
                        )
                    lines.append(jnp.concatenate(line, 1))
                parts[part][0].append(jnp.concatenate(lines, 0))
                parts[part][1].append(head_values[:seen])
        for part in range(2):
            out_ref[part * half : (part + 1) * half, spot] = jnp.dot(
                jnp.concatenate(parts[part][0], 1),
                jnp.concatenate(parts[part][1], 0),
                preferred_element_type=F32,
            )
    finish()


def front_kernel(head_size, slot_cap, *refs):
    lengths_ref, rel_ref, cand_ref, events_hbm, w_ref = refs[:5]
    sent_ref, hits_ref, kept_hbm, attended_hbm, bottom_hbm = refs[5:10]
    events_ref, w_buf, pair_buf, out_buf, mask_ref, in_sems, out_sems = refs[10:]
    rows, hidden = events_ref.shape
    half = rows // 2
    step = hidden // 2
    arrival = pltpu.make_async_copy(events_hbm, events_ref, in_sems.at[8])
    arrival.start()
    order = [2, 3, 6, 7, 4, 5, 0, 1]
    arrivals = [
        pltpu.make_async_copy(
            w_ref.at[:, pl.ds(part * step, step)],
            w_buf.at[:, pl.ds(part * step, step)],
            in_sems.at[part],
        )
        for part in order
    ]
    bottom = pltpu.make_async_copy(events_ref.at[pl.ds(half, half)], bottom_hbm, out_sems.at[0])
    kept = pltpu.make_async_copy(pair_buf.at[:, pl.ds(0, 2 * hidden)], kept_hbm, out_sems.at[1])
    attended = pltpu.make_async_copy(out_buf, attended_hbm, out_sems.at[2])
    ahead = 2
    for copy in arrivals[:ahead]:
        copy.start()
    arrival.wait()
    bottom.start()
    normed = centered(events_ref[...].astype(F32)).astype(BF16)
    for num, part in enumerate(order):
        arrivals[num].wait()
        if num + ahead < len(arrivals):
            arrivals[num + ahead].start()
        spot = slice(part * step, (part + 1) * step)
        value = jnp.dot(normed, w_buf[:, spot], preferred_element_type=F32)
        pair_buf[:, spot] = silu_of_half(0.5 * value).astype(BF16)
    kept.start()
    sent_ref[...] = requested_rows(slot_cap, cand_ref, events_ref[...])
    hits_ref[...] = slot_hits(slot_cap, rows, cand_ref)
    own_attention(head_size, lengths_ref, rel_ref, pair_buf, mask_ref, out_buf, attended.start)
    for copy in (bottom, kept, attended):
        copy.wait()


def picks_kernel(head_size, *refs):
    lengths_ref, lists_ref, rel_ref, projected_ref, before_ref = refs[:5]
    far_ref, far_twin_ref, own_twin_ref, across_ref, across_twin_ref = refs[5:10]
    passed_ref, passed_twin_ref, over_ref, over_twin_ref, w_ref = refs[10:15]
    events_hbm, next_ref, w_out_ref = refs[15:18]
    layer_hbm, score_ref = refs[18:20]
    acc_ref, q_ref, rows_ref, w_buf, pair_ref, mask_ref, near_ref = refs[20:27]
    sems, out_buf, gate_ref, events_ref, layer_ref, layer_sems = refs[27:]
    me = lax.axis_index("ctx")
    count = lax.axis_size("ctx")
    rows, hidden = q_ref.shape
    half = rows // 2
    picks = lists_ref.shape[1]
    head_count, _ = rel_ref.shape
    second = lax.rem(me, 2) == 1
    first = jnp.logical_not(second)
    upper = lax.rem(me, 4) >= 2
    lower = jnp.logical_not(upper)

    copies = []
    for pick in range(picks):
        away = lists_ref[0, pick]
        crossed = ((away == 1) & first) | ((away == 3) & second)
        target = rows_ref.at[pl.ds(pick * rows, rows)]
        head = rows_ref.at[pl.ds(pick * rows, half)]
        tail = rows_ref.at[pl.ds(pick * rows + half, half)]
        sources = [
            (away == 4, far_ref, target),
            ((away == 3) & first, far_twin_ref, target),
            ((away == 1) & second, own_twin_ref, target),
            ((away == 2) & upper, across_ref, head),
            ((away == 2) & lower, passed_ref, head),
            (away == 2, over_ref, tail),
            (crossed & upper, across_twin_ref, head),
            (crossed & lower, passed_twin_ref, head),
            (crossed, over_twin_ref, tail),
        ]
        for flag, source, spot in sources:

            @pl.when(flag)
            def _():
                pltpu.make_async_copy(source, spot, sems.at[pick]).start()

        copies.append(pltpu.make_async_copy(far_ref, target, sems.at[pick]))
    step = hidden // 2
    parts = 2 * hidden // step
    later = [
        (w_ref.at[:, pl.ds(2 * hidden + part * step, step)], w_buf.at[:, pl.ds(part * step, step)])
        for part in range(parts)
    ]
    later.append((projected_ref.at[:, pl.ds(hidden, hidden)], q_ref))
    later.append((before_ref, acc_ref))
    later.append((w_out_ref, out_buf))
    later.append((projected_ref.at[:, pl.ds(0, hidden)], gate_ref))
    later.append((events_hbm, events_ref))
    later = [
        pltpu.make_async_copy(source, target, sems.at[picks + num])
        for num, (source, target) in enumerate(later)
    ]
    for copy in copies:
        copy.wait()
    for copy in later[:parts]:
        copy.start()
    normed = centered(rows_ref[...].astype(F32)).astype(BF16)
    for part in range(parts):
        later[part].wait()
        if part == 0:
            for copy in later[parts:]:
                copy.start()
        columns = pl.ds(part * step, step)
        value = jnp.dot(normed, w_buf[:, columns], preferred_element_type=F32)
        pair_ref[:, columns] = silu_of_half(0.5 * value).astype(BF16)
    later[parts].wait()
    later[parts + 1].wait()

    base = time_base(me, count, rows)
    first_start = starts_of(base, lengths_ref)
    gap = iota((LANES, LANES), 0) - iota((LANES, LANES), 1)
    width = 4 * head_size
    scaled = head_rows(head_size, width, 0.5 * head_size**-0.5)
    chosen = head_rows(head_size, width, 1.0)
    tiles = rows // LANES

    @pl.loop(0, picks)
    def _(pick):
        away = lists_ref[0, pick]
        block = lax.rem(me - away + count, count)
        key_base = time_base(block, count, rows)
        useful = (key_base < base) & (key_base + rows - 1 >= first_start)

        @pl.when(useful)
        def _():
            start = starts_of(base + iota((rows, LANES), 0), lengths_ref)
            for tile in range(tiles):
                key_time = key_base + tile * LANES + iota((rows, LANES), 1)
                mask_ref[:, tile * LANES : (tile + 1) * LANES] = jnp.where(
                    key_time >= start, 0.0, BLOCKED
                )
            lows, highs = {}, {}
            for diff in range(1 - tiles, tiles):
                delta = away * rows + diff * LANES
                bucket, power = jnp.int32(8), jnp.int32(0)
                for degree in range(8, rel_ref.shape[1] - 1):
                    bucket = bucket + (delta >= 2**degree).astype(jnp.int32)
                    power = power + (delta == 2**degree).astype(jnp.int32)
                highs[diff] = bucket
                lows[diff] = bucket - power
            special = 1 - tiles

            @pl.when(away == 1)
            def _():
                @pl.loop(0, head_count)
                def _(head):
                    near_ref[head] = bias_chain(gap + LANES, rel_ref, head, 1, 1, 8)

            @pl.when(away != 1)
            def _():
                @pl.loop(0, head_count)
                def _(head):
                    near_ref[head] = jnp.full(
                        gap.shape, half_bias(rel_ref, head, highs[special]), F32
                    )

            key_rows = pl.ds(pl.multiple_of(pick * rows, rows), rows)
            for group in range(hidden // width):
                columns = slice(group * width, (group + 1) * width)
                queries = q_ref[:, columns]
                values = pair_ref[key_rows, columns]
                keys = pair_ref[key_rows, hidden + group * width : hidden + (group + 1) * width]
                weights, stacked = [], []
                for num in range(width // head_size):
                    head = group * (width // head_size) + num
                    scores = lax.dot_general(
                        queries * scaled[num], keys, NT, preferred_element_type=F32
                    )
                    lines = []
                    for q_tile in range(tiles):
                        line = []
                        for k_tile in range(tiles):
                            diff = q_tile - k_tile
                            if diff == special:
                                bias = near_ref[head]
                            elif diff in (0, 2 - tiles):
                                bias = jnp.where(
                                    gap >= 0,
                                    half_bias(rel_ref, head, highs[diff]),
                                    half_bias(rel_ref, head, lows[diff]),
                                )
                            else:
                                bias = half_bias(rel_ref, head, highs[diff])
                            spot = (
                                slice(q_tile * LANES, (q_tile + 1) * LANES),
                                slice(k_tile * LANES, (k_tile + 1) * LANES),
                            )
                            line.append(
                                silu_of_half(scores[spot] + bias + mask_ref[spot]).astype(BF16)
                            )
                        lines.append(jnp.concatenate(line, 1))
                    weights.append(jnp.concatenate(lines, 0))
                    stacked.append(values * chosen[num])
                acc_ref[:, columns] += jnp.dot(
                    jnp.concatenate(weights, 1),
                    jnp.concatenate(stacked, 0),
                    preferred_element_type=F32,
                )

    diagonal = iota((LANES, LANES), 0) == iota((LANES, LANES), 1)
    for copy in later[parts + 2 :]:
        copy.wait()
    scale = hidden**-0.5
    total = count * rows
    departures = []
    gated = (centered(acc_ref[...]) * gate_ref[...].astype(F32)).astype(BF16)
    mixed = jnp.dot(gated, out_buf[...], preferred_element_type=F32)
    for part in range(2):
        block_rows = slice(part * half, (part + 1) * half)
        layer = events_ref[block_rows].astype(F32) + mixed[block_rows]
        layer = layer.astype(BF16)
        layer_ref[block_rows] = layer
        leaving = pltpu.make_async_copy(
            layer_ref.at[pl.ds(part * half, half)],
            layer_hbm.at[pl.ds(part * half, half)],
            layer_sems.at[part],
        )
        leaving.start()
        departures.append(leaving)
        following = pltpu.roll(events_ref[block_rows].astype(F32), half - 1, 0)
        if part == 0:
            after = events_ref[half : half + 16][:1].astype(F32)
        else:
            after = next_ref[...].astype(F32)
        following = jnp.where(iota((half, hidden), 0) == half - 1, after, following)
        inner = jnp.sum(layer.astype(F32) * following, 1, keepdims=True) * scale
        for tile in range(half // LANES):
            spot = inner[tile * LANES : (tile + 1) * LANES]
            line = jnp.sum(jnp.where(diagonal, spot, 0.0), 0, keepdims=True)
            offset = part * half + tile * LANES
            coming = base + offset + 1 + iota((1, LANES), 1)
            same = coming < total
            end = jnp.int32(0)
            for user in range(lengths_ref.shape[0]):
                end = end + lengths_ref[user]
                same = same & (coming != end)
            score_ref[offset // LANES : offset // LANES + 1] = jnp.where(same, line, 0.0)
    for leaving in departures:
        leaving.wait()


def table_kernel(layer_hbm, flat_hbm, hits_ref, table_ref, layer_ref, flat_ref, sems):
    flat_arrival = pltpu.make_async_copy(flat_hbm, flat_ref, sems.at[0])
    flat_arrival.start()
    arrival = pltpu.make_async_copy(layer_hbm, layer_ref, sems.at[1])
    arrival.start()
    flat_arrival.wait()
    listed = jnp.dot(hits_ref[...], flat_ref[...], preferred_element_type=F32).astype(BF16)
    arrival.wait()
    scores = lax.dot_general(layer_ref[...], listed, NT, preferred_element_type=F32)
    table_ref[...] = scores * layer_ref.shape[1] ** -0.5


def smem():
    return pl.BlockSpec(memory_space=pltpu.SMEM)


def vmem():
    return pl.BlockSpec(memory_space=pltpu.VMEM)


def hbm():
    return pl.BlockSpec(memory_space=pltpu.HBM)


def anywhere():
    return pl.BlockSpec(memory_space=pl.ANY)


def placed(value):
    return pltpu.with_memory_space_constraint(value, pltpu.HBM)


def params(mebibytes, *semantics):
    return pltpu.CompilerParams(
        dimension_semantics=semantics or None, vmem_limit_bytes=mebibytes * 2**20
    )


def shards(events, w_in, w_out, rel_bias, lengths, block_lists, candidates):
    rows, hidden = events.shape
    head_count = rel_bias.shape[0]
    head_size = hidden // head_count
    count = lax.axis_size("ctx")
    wanted = candidates.shape[1]
    slot_cap = 2 * wanted // count
    slots = count * slot_cap
    half = rows // 2
    width = 4 * head_size
    picks = block_lists.shape[1]

    ring = range(count)
    across_pairs = [(s, s ^ 2) for s in ring]
    over_pairs = [(s, (s + 2) % count) for s in ring]
    far_pairs = [(s, (s + 4) % count) for s in ring]
    passing_pairs = [(s, (s + 4) % count) for s in ring if s % 4 < 2]
    back_pairs = [(s, (s - 1) % count) for s in ring]
    up_pairs = [(s, s + 1) for s in ring if s % 2 == 0]
    down_pairs = [(s, s - 1) for s in ring if s % 2 == 1]
    twin_pairs = [(s, s ^ 1) for s in ring]
    upper_twins = [(s, s ^ 1) for s in ring if s % 4 >= 2]
    lower_twins = [(s, s ^ 1) for s in ring if s % 4 < 2]

    next_first = passed_along(events[:1], back_pairs)
    own_twin = passed_along(events, up_pairs)
    across = passed_along(events[:half], across_pairs)
    far = passed_along(events, far_pairs)

    fetched, hits, kept, attended, bottom = pl.pallas_call(
        functools.partial(front_kernel, head_size, slot_cap),
        out_shape=(
            jax.ShapeDtypeStruct((slots, hidden), BF16),
            jax.ShapeDtypeStruct((wanted, slots), BF16),
            pltpu.HBM((rows, 2 * hidden), BF16),
            pltpu.HBM((rows, hidden), F32),
            pltpu.HBM((half, hidden), BF16),
        ),
        in_specs=[smem(), smem(), vmem(), hbm(), hbm()],
        out_specs=(vmem(), vmem(), hbm(), hbm(), hbm()),
        scratch_shapes=[
            pltpu.VMEM((rows, hidden), BF16),
            pltpu.VMEM((hidden, 4 * hidden), BF16),
            pltpu.VMEM((rows, 4 * hidden), BF16),
            pltpu.VMEM((rows, hidden), F32),
            pltpu.VMEM((rows, rows), F32),
            pltpu.SemaphoreType.DMA((9,)),
            pltpu.SemaphoreType.DMA((3,)),
        ],
        compiler_params=params(48),
        cost_estimate=pl.CostEstimate(
            flops=14 * 10**9, bytes_accessed=2**23, transcendentals=0
        ),
        name="front",
    )(placed(lengths), placed(rel_bias), placed(candidates), placed(events), placed(w_in))

    across, kept = lax.optimization_barrier((across, kept))
    far, attended = lax.optimization_barrier((far, attended))
    passed = passed_along(across, passing_pairs)
    over = passed_along(bottom, over_pairs)
    over_done, passed_done, fetched = lax.optimization_barrier((over, passed, fetched))
    across_twin = passed_along(across, upper_twins)
    over_twin = passed_along(over_done, twin_pairs)
    far_twin = passed_along(far, down_pairs)
    passed_twin = passed_along(passed_done, lower_twins)
    arrived = lax.all_to_all(
        fetched.reshape(count, slot_cap, hidden), "ctx", split_axis=0, concat_axis=0, tiled=True
    ).reshape(slots, hidden)

    parts = 4
    operands = [placed(kept), placed(attended), far, far_twin, own_twin, across]
    operands += [across_twin, passed_done, passed_twin, over_done, over_twin, placed(w_in), placed(events)]
    layer_output, next_score = pl.pallas_call(
        functools.partial(picks_kernel, head_size),
        out_shape=(
            pltpu.HBM((rows, hidden), BF16),
            jax.ShapeDtypeStruct((rows // LANES, LANES), F32),
        ),
        in_specs=[smem()] * 3 + [hbm()] * 2 + [anywhere()] * 9 + [hbm()] * 2 + [vmem(), hbm()],
        out_specs=(hbm(), vmem()),
        scratch_shapes=[
            pltpu.VMEM((rows, hidden), F32),
            pltpu.VMEM((rows, hidden), BF16),
            pltpu.VMEM((picks * rows, hidden), BF16),
            pltpu.VMEM((hidden, 2 * hidden), BF16),
            pltpu.VMEM((picks * rows, 2 * hidden), BF16),
            pltpu.VMEM((rows, rows), F32),
            pltpu.VMEM((head_count, LANES, LANES), F32),
            pltpu.SemaphoreType.DMA((picks + parts + 5,)),
            pltpu.VMEM((hidden, hidden), BF16),
            pltpu.VMEM((rows, hidden), BF16),
            pltpu.VMEM((rows, hidden), BF16),
            pltpu.VMEM((rows, hidden), BF16),
            pltpu.SemaphoreType.DMA((2,)),
        ],
        compiler_params=params(50),
        cost_estimate=pl.CostEstimate(
            flops=20 * 10**9, bytes_accessed=2**23, transcendentals=0
        ),
        name="picks",
    )(lengths, block_lists, rel_bias, *operands, next_first, placed(w_out))
    table = pl.pallas_call(
        table_kernel,
        out_shape=jax.ShapeDtypeStruct((rows, wanted), F32),
        in_specs=[hbm(), anywhere(), vmem()],
        out_specs=vmem(),
        scratch_shapes=[
            pltpu.VMEM((rows, hidden), BF16),
            pltpu.VMEM((slots, hidden), BF16),
            pltpu.SemaphoreType.DMA((2,)),
        ],
        compiler_params=params(10),
        cost_estimate=pl.CostEstimate(flops=10**9, bytes_accessed=2**21, transcendentals=0),
        name="table",
    )(placed(layer_output), arrived, hits)
    return (layer_output, next_score.reshape(rows), table)


def solution(mesh):
    in_specs = (
        P(("groups", "ctx"), None),
        P(),
        P(),
        P(),
        P("groups"),
        P(("groups", "ctx"), None),
        P("groups", None),
    )
    out_specs = (P(("groups", "ctx"), None), P(("groups", "ctx")), P(("groups", "ctx"), None))
    return jax.shard_map(shards, mesh=mesh, in_specs=in_specs, out_specs=out_specs, check_vma=False)
```
